256 devices in a mesh: row: 32 (over z, y_lo, core), col: 8 (over x, y_hi).
Axes of the slice: x: 4, y: 4 (y_hi: 2, y_lo: 2; y = y_hi * 2 + y_lo), z: 8, core: 2. Of those that a mesh axis runs over, the one named last changes fastest.
Arguments:
- acts: bfloat16 [1024, 16384], P(None, 'col'), may hold values from -6 to 6
- grads: bfloat16 [1024, 16384], P(None, 'row'), may hold values from -0.1875 to 0.1875
- row_roots: bfloat16 [16384, 1024], P('row'), as said below
- col_stats: float32 [1024, 16384], P('row', 'col'), as said below
Outputs:
- update: bfloat16 [16384, 16384], P('row', 'col')
- new_stats: float32 [1024, 16384], P('row', 'col')
- new_roots: float32 [1024, 16384], P('row', 'col')
The draws below stay inside these ranges and needn't reach their ends.
Inputs may be any that keep to these rules, and one draw needn't show every extreme that they name: `col_stats`: each block of 1024 columns is symmetric positive definite. `row_roots`: each block of 1024 rows is symmetric.
All inputs are finite; a program needn't handle non-finite values.
Results may differ from the reference program's by a relative error of at most 0.0015.
The reference program's roundings to bfloat16 on the way (of `grad`, `whitened` and `roots_half`) count: a program that leaves them out, or rounds other values in their place, can miss the bound.
Values may be sent and summed in bfloat16 or wider, within the bound.
No kernel may reach another device: no remote copies, remote signals or barrier semaphores. Data moves between devices by JAX's collectives and lax.ppermute only.
A program may use at most 128 MiB of HBM per device.

```python
import jax
import jax.numpy as jnp
from jax import lax

BLK = 1024
TOK = 1024
DOUT = 16384
DIN = 16384


def symmetric_blocks(key, count, size, lower, upper):
    key_diag, key_noise = jax.random.split(key)
    diagonal = jnp.exp(jax.random.uniform(key_diag, (count, size), jnp.float32, jnp.log(lower), jnp.log(upper)))
    noise = jax.random.normal(key_noise, (count, size, size), jnp.float32) * (0.3 / jnp.sqrt(1.0 * size))
    sym = 0.5 * (noise + jnp.swapaxes(noise, 1, 2))
    inner = jnp.eye(size, dtype=jnp.float32)[None] + sym
    roots_diag = jnp.sqrt(diagonal)
    return roots_diag[:, :, None] * inner * roots_diag[:, None, :]


def draw_row_roots(key, part):
    blocks = symmetric_blocks(jax.random.fold_in(key, 11), DOUT // BLK, BLK, 0.5, 2.0)
    return blocks.reshape(DOUT, BLK).astype(jnp.bfloat16)


def draw_col_stats(key, part):
    blocks = symmetric_blocks(jax.random.fold_in(key, 23), DIN // BLK, BLK, 1.0, 3.0)
    return blocks.transpose(1, 0, 2).reshape(BLK, DIN)


def block_scale(rng, extent, pieces, least, high):
    level = 1.0
    for axis_at, blocks in pieces:
        steps = jax.random.uniform(jax.random.fold_in(jax.random.fold_in(rng, 6), axis_at), (blocks,), jnp.float32, least / len(pieces), high / len(pieces))
        level = level * jnp.repeat(jnp.exp(steps), extent[axis_at] // blocks).reshape((-1,) + (1,) * (len(extent) - 1 - axis_at))
    return level


def scatter_about(key, dims, spread, limit, shards=(), kind=jnp.bfloat16):
    array = spread * jax.random.normal(key, dims, jnp.float32)
    if shards:
        array = array * block_scale(key, dims, shards, -0.22, 0.18)
    return jnp.clip(array, -limit, limit).astype(kind)


def setup_inputs(seed: int = 0) -> dict:
    streams_of = jax.random.split(jax.random.key(seed), 5)
    acts = scatter_about(streams_of[0], (TOK, DIN), 1.0, 6.0, ((1, 8),))
    grads = scatter_about(streams_of[1], (TOK, DOUT), TOK ** -0.5, 0.1875, ((1, 32),))
    row_roots = draw_row_roots(jax.random.fold_in(streams_of[4], 71), 0)
    col_stats = draw_col_stats(jax.random.fold_in(streams_of[4], 71), 0)
    return dict(acts=acts, grads=grads, row_roots=row_roots, col_stats=col_stats)


decay_rate = 0.75
damping = 0.001
epsilon = 1e-06

def inverse_root(stat):
    size = stat.shape[0]
    identity = jnp.eye(size, dtype=stat.dtype)
    shifted = stat + damping * identity
    norm_scale = 2.0 * jnp.trace(shifted) / size
    start_iterate = shifted / norm_scale
    first_factor = 1.5 * identity - 0.5 * start_iterate
    second_iterate = jnp.dot(start_iterate, first_factor, precision=lax.Precision.HIGHEST)
    product_full = jnp.dot(first_factor, second_iterate, precision=lax.Precision.HIGHEST)
    second_factor = 1.5 * identity - 0.5 * product_full
    root_full = jnp.dot(second_factor, first_factor, precision=lax.Precision.HIGHEST)
    return root_full / jnp.sqrt(norm_scale)

def reference(acts, grads, row_roots, col_stats):
    contract_first = (((0,), (0,)), ((), ()))
    grad = lax.dot_general(grads, acts, contract_first, preferred_element_type=jnp.float32).astype(jnp.bfloat16)
    row_blocks = DOUT // BLK
    col_blocks = DIN // BLK
    roots_three = row_roots.reshape(row_blocks, BLK, BLK)
    grad_three = grad.reshape(row_blocks, BLK, DIN)

    def whiten(pair):
        return jnp.dot(pair[0], pair[1], preferred_element_type=jnp.float32).astype(jnp.bfloat16)
    whitened = lax.map(whiten, (roots_three, grad_three)).reshape(DOUT, DIN)
    columns = whitened.reshape(DOUT, col_blocks, BLK).transpose(1, 0, 2)
    old_three = col_stats.reshape(BLK, col_blocks, BLK).transpose(1, 0, 2)
    mix = (1.0 - decay_rate) / DOUT

    def column_block(pair):
        wcols, old = pair
        part = lax.dot_general(wcols, wcols, contract_first, preferred_element_type=jnp.float32)
        stat = decay_rate * old + mix * part
        return (stat, inverse_root(stat))
    stats_three, roots_new = lax.map(column_block, (columns, old_three))
    roots_half = roots_new.astype(jnp.bfloat16)

    def precondition(pair):
        return jnp.dot(pair[0], pair[1], preferred_element_type=jnp.float32)
    product = lax.map(precondition, (columns, roots_half))
    product = product.transpose(1, 0, 2).reshape(DOUT, DIN)
    grad_square = jnp.sum(jnp.square(grad.astype(jnp.float32)))
    prod_square = jnp.sum(jnp.square(product))
    update = (product * jnp.sqrt(grad_square / (prod_square + epsilon))).astype(jnp.bfloat16)
    new_stats = stats_three.transpose(1, 0, 2).reshape(BLK, DIN)
    new_roots = roots_new.transpose(1, 0, 2).reshape(BLK, DIN)
    return (update, new_stats, new_roots)
```

```python
import jax
import jax.numpy as jnp
from jax import lax
from jax.sharding import Mesh, PartitionSpec as P
from jax.experimental import pallas as pl
from jax.experimental.pallas import tpu as pltpu

decay_rate = 0.75
damping = 0.001
epsilon = 1e-06
TILE = 256
SLAB = 128
DISTANCES = 5
f32 = jnp.float32
bf16 = jnp.bfloat16


def tdot(a, b):
    return lax.dot_general(a, b, (((0,), (0,)), ((), ())), preferred_element_type=f32)


def dot(a, b):
    return jnp.dot(a, b, preferred_element_type=f32)


def front_kernel(ids, acts, g_own, g_other, r_own, r_other, white, gsq, *rest):
    chunks, (grad, wide) = rest[:-2], rest[-2:]
    core, z = ids[0], ids[1]
    half = g_own.shape[1]
    size = acts.shape[1]
    slabs = size // SLAB
    total = jnp.float32(0)
    for g, who in ((g_own, core), (g_other, 1 - core)):
        first = pl.multiple_of(who * half, half)
        for j in range(size // TILE):
            cols = pl.ds(j * TILE, TILE)
            t = tdot(g[...], acts[:, cols]).astype(bf16)
            grad[pl.ds(first, half), cols] = t
            total += jnp.sum(jnp.square(t.astype(f32)))
    gsq[0, 0] = total
    for r, who in ((r_own, core), (r_other, 1 - core)):
        first = pl.multiple_of(who * half, half)
        for j in range(size // TILE):
            cols = pl.ds(j * TILE, TILE)
            t = dot(r[...], grad[:, cols]).astype(bf16)
            white[pl.ds(first, half), cols] = t
            wide[pl.ds(first, half), cols] = t
            if j * TILE < (DISTANCES - 1) * SLAB:
                wide[pl.ds(first, half), pl.ds(size + j * TILE, TILE)] = t
    for k in range(slabs):
        first = pl.multiple_of(lax.rem(z + k, slabs) * SLAB, SLAB)
        chunks[k][...] = tdot(wide[:, pl.ds(first, SLAB)], wide[:, pl.ds(first, DISTANCES * SLAB)])


def front(ids, acts, g_own, g_other, r_own, r_other):
    tok, half = g_own.shape
    size = r_own.shape[1]
    slabs = size // SLAB
    whole = lambda shape: pl.BlockSpec(shape, lambda i, s: (0, 0))
    flops = 2 * size * size * (tok + size) + 2 * size * size * DISTANCES * SLAB
    return pl.pallas_call(
        front_kernel,
        out_shape=[
            jax.ShapeDtypeStruct((size, size), bf16),
            jax.ShapeDtypeStruct((1, 1), f32),
        ]
        + [jax.ShapeDtypeStruct((SLAB, DISTANCES * SLAB), f32)] * slabs,
        grid_spec=pltpu.PrefetchScalarGridSpec(
            num_scalar_prefetch=1,
            grid=(1,),
            in_specs=[
                pl.BlockSpec((tok, size), lambda i, s: (0, s[0])),
                whole((tok, half)),
                whole((tok, half)),
                whole((half, size)),
                whole((half, size)),
            ],
            out_specs=[
                whole((size, size)),
                pl.BlockSpec(memory_space=pltpu.SMEM),
            ]
            + [whole((SLAB, DISTANCES * SLAB))] * slabs,
            scratch_shapes=[
                pltpu.VMEM((size, size), bf16),
                pltpu.VMEM((size, size + (DISTANCES - 1) * SLAB), bf16),
            ],
        ),
        compiler_params=pltpu.CompilerParams(vmem_limit_bytes=56 << 20),
        cost_estimate=pl.CostEstimate(flops=flops, bytes_accessed=12 << 20, transcendentals=0),
        name="front",
    )(ids, acts, g_own, g_other, r_own, r_other)


def halves(x):
    high = x.astype(bf16)
    return high, (x - high.astype(f32)).astype(bf16)


def root_kernel(ids, *refs):
    slabs = 8
    chunks = refs[:slabs]
    white, part, prod, stat_rows, root_rows, psq = refs[slabs : slabs + 6]
    y, yh, yl, zh, zl, qh, ql, rh, root = refs[slabs + 6 :]
    z, sub = ids[1], ids[2]
    size = white.shape[1]
    rows64 = stat_rows.shape[0]
    own = pl.multiple_of(z * SLAB + sub * rows64, rows64)

    def at(k):
        return pl.ds(pl.multiple_of(lax.rem(z + k, slabs) * SLAB, SLAB), SLAB)

    diag = lax.broadcasted_iota(jnp.int32, (SLAB, SLAB), 0) == lax.broadcasted_iota(
        jnp.int32, (SLAB, SLAB), 1
    )
    trace = jnp.float32(0)
    for k in range(slabs):
        for d in range(DISTANCES):
            block = chunks[k][:, d * SLAB : (d + 1) * SLAB]
            y[at(k), at(k + d)] = block
            if d == 0:
                trace += jnp.sum(jnp.where(diag, block + damping, 0.0))
            elif d < DISTANCES - 1:
                y[at(k + d), at(k)] = block.T
    stat_rows[...] = y[pl.ds(own, rows64), :]
    norm = 2.0 * trace / size
    inverse = 1.0 / norm
    for i in range(size // TILE):
        rows = pl.ds(i * TILE, TILE)
        eye = (
            lax.broadcasted_iota(jnp.int32, (TILE, size), 0) + i * TILE
            == lax.broadcasted_iota(jnp.int32, (TILE, size), 1)
        )
        v = (y[rows, :] + jnp.where(eye, damping, 0.0)) * inverse
        y[rows, :] = v
        yh[rows, :], yl[rows, :] = halves(v)
    for j in range(size // TILE):
        cols = pl.ds(j * TILE, TILE)
        eye = (
            lax.broadcasted_iota(jnp.int32, (size, TILE), 0)
            == lax.broadcasted_iota(jnp.int32, (size, TILE), 1) + j * TILE
        )
        v = dot(yh[...], yh[:, cols]) + (dot(yh[...], yl[:, cols]) + dot(yl[...], yh[:, cols]))
        zh[:, cols], zl[:, cols] = halves(v)
        q = jnp.where(eye, 1.6875, 0.0) - 0.5625 * y[:, cols] + 0.0625 * v
        qh[:, cols], ql[:, cols] = halves(q)
    scale = lax.rsqrt(jnp.full((1, 1), norm, f32))
    for j in range(size // TILE):
        cols = pl.ds(j * TILE, TILE)
        eye = (
            lax.broadcasted_iota(jnp.int32, (size, TILE), 0)
            == lax.broadcasted_iota(jnp.int32, (size, TILE), 1) + j * TILE
        )
        v = dot(zh[...], qh[:, cols]) + (dot(zh[...], ql[:, cols]) + dot(zl[...], qh[:, cols]))
        v = (jnp.where(eye, 2.25, 0.0) - 2.4375 * y[:, cols] + v) * scale
        root[:, cols] = v
        rh[:, cols] = v.astype(bf16)
    root_rows[...] = root[pl.ds(own, rows64), :]
    acc = jnp.zeros((SLAB, size), f32)
    for d in range(DISTANCES):
        weight = 2.0 if 0 < d < DISTANCES - 1 else 1.0
        high, low = halves(part[:, d * SLAB : (d + 1) * SLAB] * weight)
        acc += dot(high, rh[at(d), :]) + dot(low, rh[at(d), :])
    psq[0, 0] = jnp.sum(acc * rh[at(0), :].astype(f32))
    for j in range(size // TILE):
        cols = pl.ds(j * TILE, TILE)
        prod[:, cols] = dot(white[...], rh[:, cols])


def root(ids, chunks, white, part, rows64):
    slabs = len(chunks)
    size = white.shape[1]
    whole = lambda shape: pl.BlockSpec(shape, lambda i, s: (0, 0))
    square = lambda kind: pltpu.VMEM((size, size), kind)
    return pl.pallas_call(
        root_kernel,
        out_shape=[
            jax.ShapeDtypeStruct((size, size), f32),
            jax.ShapeDtypeStruct((rows64, size), f32),
            jax.ShapeDtypeStruct((rows64, size), f32),
            jax.ShapeDtypeStruct((1, 1), f32),
        ],
        grid_spec=pltpu.PrefetchScalarGridSpec(
            num_scalar_prefetch=1,
            grid=(1,),
            in_specs=[whole((SLAB, DISTANCES * SLAB))] * slabs
            + [whole((size, size)), whole((SLAB, DISTANCES * SLAB))],
            out_specs=[
                whole((size, size)),
                whole((rows64, size)),
                whole((rows64, size)),
                pl.BlockSpec(memory_space=pltpu.SMEM),
            ],
            scratch_shapes=[square(f32)] + [square(bf16)] * 7 + [square(f32)],
        ),
        compiler_params=pltpu.CompilerParams(vmem_limit_bytes=60 << 20),
        cost_estimate=pl.CostEstimate(
            flops=2 * size**3 * 7, bytes_accessed=12 << 20, transcendentals=0
        ),
        name="root",
    )(ids, *chunks, white, part)


def shift(x, by):
    count = lax.axis_size("z")
    return lax.ppermute(x, "z", [(i, (i + by) % count) for i in range(count)])


def swap(x, axis):
    return lax.ppermute(x, axis, [(0, 1), (1, 0)])


def by_index(which, mine, other, dim):
    return jnp.where(
        which == 0, jnp.concatenate([mine, other], dim), jnp.concatenate([other, mine], dim)
    )


def gather_stats(col_stats, core, sub, z, size):
    rows = col_stats.shape[0]
    mine = lax.dynamic_slice_in_dim(col_stats, core * size, size, 1)
    theirs = lax.dynamic_slice_in_dim(col_stats, (1 - core) * size, size, 1)
    chip = by_index(core, mine, swap(theirs, "core"), 0)
    wide = jnp.concatenate([chip, chip[:, : (DISTANCES - 1) * SLAB]], 1)
    packed = lax.dynamic_slice(wide, (0, z * SLAB), (2 * rows, DISTANCES * SLAB))
    return by_index(sub, packed, swap(packed, "yl"), 0)


def reduce_ring(parts):
    cut = SLAB // 2
    up = shift(parts[4][:cut], 1)
    down = shift(parts[4][cut:], -1)
    up = jnp.concatenate([parts[3][:cut] + up, parts[3][cut:]], 0)
    down = jnp.concatenate([parts[5][:cut], parts[5][cut:] + down], 0)
    up, down = shift(up, 1), shift(down, -1)
    up, down = parts[2] + up, parts[6] + down
    up, down = shift(up, 1), shift(down, -1)
    up, down = parts[1] + up, parts[7] + down
    up, down = shift(up, 1), shift(down, -1)
    return parts[0] + up + down


def gather_ring(own):
    cut = SLAB // 2
    chunks = [own] + [None] * 7
    up = down = own
    for step in range(1, 4):
        up, down = shift(up, 1), shift(down, -1)
        chunks[8 - step], chunks[step] = up, down
    up, down = shift(up[:cut], 1), shift(down[cut:], -1)
    chunks[4] = jnp.concatenate([up, down], 0)
    return chunks


def exchange_rows(x, core):
    rows = x.shape[0] // 2
    mine = lax.dynamic_slice_in_dim(x, core * rows, rows, 0)
    theirs = lax.dynamic_slice_in_dim(x, (1 - core) * rows, rows, 0)
    return by_index(core, mine, swap(theirs, "core"), 1)


def shards(acts, grads, row_roots, col_stats):
    size = row_roots.shape[1]
    z, sub, core = lax.axis_index("z"), lax.axis_index("yl"), lax.axis_index("core")
    ids = jnp.stack([core, z, sub]).astype(jnp.int32)
    total_rows = grads.shape[1] * lax.axis_size(("z", "yl", "core"))
    mix = (1.0 - decay_rate) / total_rows

    grads_other, roots_other = swap(grads, "core"), swap(row_roots, "core")
    old = gather_stats(col_stats, core, sub, z, size)
    white, grad_square, *parts = front(ids, acts, grads, grads_other, row_roots, roots_other)
    grad_square = grad_square + swap(grad_square, "yl")
    part = reduce_ring(parts)
    part = part + swap(part, "yl")
    chunks = gather_ring(decay_rate * old + mix * part)
    product, stat_rows, root_rows, prod_square = root(
        ids, chunks, white, part, 2 * col_stats.shape[0]
    )
    squares = jnp.concatenate([grad_square, prod_square], 1)
    squares = squares + swap(squares, "core")
    squares = lax.psum(squares, "z")
    squares = lax.psum(squares, ("x", "yh"))
    scale = jnp.sqrt(squares[0, 0] / (squares[0, 1] + epsilon))
    update = (exchange_rows(product, core) * scale).astype(bf16)
    return update, exchange_rows(stat_rows, core), exchange_rows(root_rows, core)


def solution(mesh):
    names = ("z", "yl", "core", "x", "yh")
    fine = Mesh(mesh.devices.reshape(8, 2, 2, 4, 2), names)
    row, col = names[:3], names[3:]
    return jax.shard_map(
        shards,
        mesh=fine,
        in_specs=(P(None, col), P(None, row), P(row, None), P(row, col)),
        out_specs=(P(row, col), P(row, col), P(row, col)),
        check_vma=False,
    )
```

```python
import jax
import jax.numpy as jnp
from jax import lax
from jax.sharding import Mesh, PartitionSpec as P
from jax.experimental import pallas as pl
from jax.experimental.pallas import tpu as pltpu

decay_rate = 0.75
damping = 0.001
epsilon = 1e-06
TILE = 256
SLAB = 128
DISTANCES = 5
f32 = jnp.float32
bf16 = jnp.bfloat16


def tdot(a, b):
    return lax.dot_general(a, b, (((0,), (0,)), ((), ())), preferred_element_type=f32)


def dot(a, b):
    return jnp.dot(a, b, preferred_element_type=f32)


def tiles(count, body):
    def step(j, carry):
        body(pl.ds(pl.multiple_of(j * TILE, TILE), TILE), j)
        return carry

    lax.fori_loop(0, count, step, 0)


def front_kernel(ids, acts, g_own, g_other, r_own, r_other, white, gsq, *rest):
    pieces, (grad, wide) = rest[:-2], rest[-2:]
    core, z = ids[0], ids[1]
    half = g_own.shape[1]
    size = acts.shape[1]
    slabs = size // SLAB
    gsq[0, 0] = 0.0
    for g, who in ((g_own, core), (g_other, 1 - core)):
        first = pl.multiple_of(who * half, half)

        def fill_grad(cols, j):
            t = tdot(g[...], acts[:, cols]).astype(bf16)
            grad[pl.ds(first, half), cols] = t
            gsq[0, 0] += jnp.sum(jnp.square(t.astype(f32)))

        tiles(size // TILE, fill_grad)
    for r, who in ((r_own, core), (r_other, 1 - core)):
        first = pl.multiple_of(who * half, half)

        def fill_white(cols, j):
            t = dot(r[...], grad[:, cols]).astype(bf16)
            white[pl.ds(first, half), cols] = t
            wide[pl.ds(first, half), cols] = t

        tiles(size // TILE, fill_white)
    wide[:, size:] = white[:, : (DISTANCES - 1) * SLAB]
    for k in range(slabs):
        first = pl.multiple_of(lax.rem(z + k, slabs) * SLAB, SLAB)
        t = tdot(wide[:, pl.ds(first, SLAB)], wide[:, pl.ds(first, DISTANCES * SLAB)])
        pieces[2 * k][...] = t[: SLAB // 2]
        pieces[2 * k + 1][...] = t[SLAB // 2 :]


def front(ids, acts, g_own, g_other, r_own, r_other):
    tok, half = g_own.shape
    size = r_own.shape[1]
    slabs = size // SLAB
    whole = lambda shape: pl.BlockSpec(shape, lambda i, s: (0, 0))
    piece = (SLAB // 2, DISTANCES * SLAB)
    flops = 2 * size * size * (tok + size) + 2 * size * size * DISTANCES * SLAB
    return pl.pallas_call(
        front_kernel,
        out_shape=[
            jax.ShapeDtypeStruct((size, size), bf16),
            jax.ShapeDtypeStruct((1, 1), f32),
        ]
        + [jax.ShapeDtypeStruct(piece, f32)] * (2 * slabs),
        grid_spec=pltpu.PrefetchScalarGridSpec(
            num_scalar_prefetch=1,
            grid=(1,),
            in_specs=[
                pl.BlockSpec((tok, size), lambda i, s: (0, s[0])),
                whole((tok, half)),
                whole((tok, half)),
                whole((half, size)),
                whole((half, size)),
            ],
            out_specs=[
                whole((size, size)),
                pl.BlockSpec(memory_space=pltpu.SMEM),
            ]
            + [whole(piece)] * (2 * slabs),
            scratch_shapes=[
                pltpu.VMEM((size, size), bf16),
                pltpu.VMEM((size, size + (DISTANCES - 1) * SLAB), bf16),
            ],
        ),
        compiler_params=pltpu.CompilerParams(vmem_limit_bytes=56 << 20),
        cost_estimate=pl.CostEstimate(flops=flops, bytes_accessed=12 << 20, transcendentals=0),
        name="front",
    )(ids, acts, g_own, g_other, r_own, r_other)


def halves(x):
    high = x.astype(bf16)
    return high, (x - high.astype(f32)).astype(bf16)


def eye_tile(shape, row, col):
    return (
        lax.broadcasted_iota(jnp.int32, shape, 0) + row
        == lax.broadcasted_iota(jnp.int32, shape, 1) + col
    )


def root_kernel(ids, gsq, *refs):
    slabs = 8
    pieces = refs[: 2 * slabs]
    white, part_a, part_b, prod_own, prod_other, stat_rows, root_rows, squares = refs[
        2 * slabs : 2 * slabs + 8
    ]
    y, yh, yl, zh, zl, qh, ql, rh, root = refs[2 * slabs + 8 :]
    core, z, sub = ids[0], ids[1], ids[2]
    size = white.shape[1]
    cut = SLAB // 2
    rows64 = stat_rows.shape[0]
    own = pl.multiple_of(z * SLAB + sub * rows64, rows64)

    def at(k):
        return pl.ds(pl.multiple_of(lax.rem(z + k, slabs) * SLAB, SLAB), SLAB)

    def part_at(k, h):
        return pl.ds(pl.multiple_of(lax.rem(z + k, slabs) * SLAB + h * cut, cut), cut)

    diagonal = eye_tile((SLAB, SLAB), 0, 0)
    trace = jnp.float32(0)
    for k in range(slabs):
        for d in range(DISTANCES):
            cols = slice(d * SLAB, (d + 1) * SLAB)
            block = jnp.concatenate([pieces[2 * k][:, cols], pieces[2 * k + 1][:, cols]], 0)
            y[at(k), at(k + d)] = block
            if d == 0:
                trace += jnp.sum(jnp.where(diagonal, block + damping, 0.0))
            elif d < DISTANCES - 1:
                y[at(k + d), at(k)] = block.T
    stat_rows[...] = y[pl.ds(own, rows64), :]
    norm = 2.0 * trace / size
    inverse = 1.0 / norm

    def fill_y(rows, i):
        eye = eye_tile((TILE, size), i * TILE, 0)
        v = (y[rows, :] + jnp.where(eye, damping, 0.0)) * inverse
        y[rows, :] = v
        yh[rows, :], yl[rows, :] = halves(v)

    tiles(size // TILE, fill_y)

    def fill_z(cols, j):
        eye = eye_tile((size, TILE), 0, j * TILE)
        v = dot(yh[...], yh[:, cols]) + (dot(yh[...], yl[:, cols]) + dot(yl[...], yh[:, cols]))
        zh[:, cols], zl[:, cols] = halves(v)
        q = jnp.where(eye, 1.6875, 0.0) - 0.5625 * y[:, cols] + 0.0625 * v
        qh[:, cols], ql[:, cols] = halves(q)

    tiles(size // TILE, fill_z)
    scale = lax.rsqrt(jnp.full((1, 1), norm, f32))

    def fill_root(cols, j):
        eye = eye_tile((size, TILE), 0, j * TILE)
        v = dot(zh[...], qh[:, cols]) + (dot(zh[...], ql[:, cols]) + dot(zl[...], qh[:, cols]))
        v = (jnp.where(eye, 2.25, 0.0) - 2.4375 * y[:, cols] + v) * scale
        root[:, cols] = v
        rh[:, cols] = v.astype(bf16)

    tiles(size // TILE, fill_root)
    root_rows[...] = root[pl.ds(own, rows64), :]
    total = jnp.float32(0)
    for h, part in ((0, part_a), (1, part_b)):
        acc = jnp.zeros((cut, size), f32)
        for d in range(DISTANCES):
            weight = 2.0 if 0 < d < DISTANCES - 1 else 1.0
            high, low = halves(part[:, d * SLAB : (d + 1) * SLAB] * weight)
            acc += dot(high, rh[at(d), :]) + dot(low, rh[at(d), :])
        total += jnp.sum(acc * rh[part_at(0, h), :].astype(f32))
    lane = lax.broadcasted_iota(jnp.int32, squares.shape, 2)
    squares[...] = jnp.where(lane == 0, gsq[0, 0], jnp.where(lane == 1, total, 0.0))
    for prod, who in ((prod_own, core), (prod_other, 1 - core)):
        rows = pl.ds(pl.multiple_of(who * (size // 2), size // 2), size // 2)

        def fill_prod(cols, j):
            prod[:, cols] = dot(white[rows, :], rh[:, cols])

        tiles(size // TILE, fill_prod)


def root(ids, gsq, pieces, white, part, rows64, peers):
    size = white.shape[1]
    whole = lambda shape: pl.BlockSpec(shape, lambda i, s: (0, 0))
    square = lambda kind: pltpu.VMEM((size, size), kind)
    piece = (SLAB // 2, DISTANCES * SLAB)
    return pl.pallas_call(
        root_kernel,
        out_shape=[
            jax.ShapeDtypeStruct((size // 2, size), f32),
            jax.ShapeDtypeStruct((size // 2, size), f32),
            jax.ShapeDtypeStruct((rows64, size), f32),
            jax.ShapeDtypeStruct((rows64, size), f32),
            jax.ShapeDtypeStruct((peers, 1, 128), f32),
        ],
        grid_spec=pltpu.PrefetchScalarGridSpec(
            num_scalar_prefetch=1,
            grid=(1,),
            in_specs=[pl.BlockSpec(memory_space=pltpu.SMEM)]
            + [whole(piece)] * len(pieces)
            + [whole((size, size)), whole(piece), whole(piece)],
            out_specs=[
                whole((size // 2, size)),
                whole((size // 2, size)),
                whole((rows64, size)),
                whole((rows64, size)),
                pl.BlockSpec((peers, 1, 128), lambda i, s: (0, 0, 0)),
            ],
            scratch_shapes=[square(f32)] + [square(bf16)] * 7 + [square(f32)],
        ),
        compiler_params=pltpu.CompilerParams(vmem_limit_bytes=60 << 20),
        cost_estimate=pl.CostEstimate(
            flops=2 * size**3 * 7, bytes_accessed=12 << 20, transcendentals=0
        ),
        name="root",
    )(ids, gsq, *pieces, white, *part)


def finish_kernel(ids, squares, own, other, update):
    sums = jnp.sum(squares[...], axis=0)
    scale = jnp.sqrt(sums[:, 0:1] / (sums[:, 1:2] + epsilon))

    @pl.when(pl.program_id(0) == 0)
    def _():
        update[...] = (own[...] * scale).astype(update.dtype)

    @pl.when(pl.program_id(0) == 1)
    def _():
        update[...] = (other[...] * scale).astype(update.dtype)


def finish(ids, squares, own, other):
    rows, size = own.shape
    return pl.pallas_call(
        finish_kernel,
        out_shape=jax.ShapeDtypeStruct((rows, 2 * size), bf16),
        grid_spec=pltpu.PrefetchScalarGridSpec(
            num_scalar_prefetch=1,
            grid=(2,),
            in_specs=[
                pl.BlockSpec(squares.shape, lambda i, s: (0, 0, 0)),
                pl.BlockSpec((rows, size), lambda i, s: (0, 0)),
                pl.BlockSpec((rows, size), lambda i, s: (0, 0)),
            ],
            out_specs=pl.BlockSpec((rows, size), lambda i, s: (0, lax.rem(s[0] + i, 2))),
        ),
        compiler_params=pltpu.CompilerParams(vmem_limit_bytes=40 << 20),
        name="finish",
    )(ids, squares, own, other)


def shift(x, by):
    count = lax.axis_size("z")
    return lax.ppermute(x, "z", [(i, (i + by) % count) for i in range(count)])


def swap(x, axis):
    return lax.ppermute(x, axis, [(0, 1), (1, 0)])


def by_index(which, mine, other, dim):
    return jnp.where(
        which == 0, jnp.concatenate([mine, other], dim), jnp.concatenate([other, mine], dim)
    )


def gather_stats(col_stats, core, sub, z, size):
    rows = col_stats.shape[0]
    mine = lax.dynamic_slice_in_dim(col_stats, core * size, size, 1)
    theirs = lax.dynamic_slice_in_dim(col_stats, (1 - core) * size, size, 1)
    chip = by_index(core, mine, swap(theirs, "core"), 0)
    wide = jnp.concatenate([chip, chip[:, : (DISTANCES - 1) * SLAB]], 1)
    packed = lax.dynamic_slice(wide, (0, z * SLAB), (2 * rows, DISTANCES * SLAB))
    return by_index(sub, packed, swap(packed, "yl"), 0)


def reduce_ring(pieces):
    def chain(h, first, by):
        held = shift(pieces[2 * first + h], by)
        for k in range(first - by, 0 if by > 0 else 8, -by):
            held = shift(pieces[2 * k + h] + held, by)
        return held

    up_a, down_b = chain(0, 4, 1), chain(1, 4, -1)
    up_b, down_a = chain(1, 3, 1), chain(0, 5, -1)
    return pieces[0] + up_a + down_a, pieces[1] + up_b + down_b


def gather_ring(own):
    pieces = list(own) + [None] * 14
    for hops in range(4):
        for h, by in ((0, 1), (1, -1), (1, 1), (0, -1)):
            if hops == 3 and (h, by) in ((1, 1), (0, -1)):
                continue
            source = -by * hops % 8
            pieces[2 * (-by * (hops + 1) % 8) + h] = shift(pieces[2 * source + h], by)
    return pieces


def exchange_rows(x, core):
    rows = x.shape[0] // 2
    mine = lax.dynamic_slice_in_dim(x, core * rows, rows, 0)
    theirs = lax.dynamic_slice_in_dim(x, (1 - core) * rows, rows, 0)
    return by_index(core, mine, swap(theirs, "core"), 1)


def shards(acts, grads, row_roots, col_stats):
    size = row_roots.shape[1]
    z, sub, core = lax.axis_index("z"), lax.axis_index("yl"), lax.axis_index("core")
    ids = jnp.stack([core, z, sub]).astype(jnp.int32)
    total_rows = grads.shape[1] * lax.axis_size(("z", "yl", "core"))
    mix = (1.0 - decay_rate) / total_rows

    grads_other, roots_other = swap(grads, "core"), swap(row_roots, "core")
    old = gather_stats(col_stats, core, sub, z, size)
    white, grad_square, *pieces = front(ids, acts, grads, grads_other, row_roots, roots_other)
    grad_square = grad_square + swap(grad_square, "yl")
    part = [p + swap(p, "yl") for p in reduce_ring(pieces)]
    cut = SLAB // 2
    stats = [decay_rate * old[h * cut : (h + 1) * cut] + mix * part[h] for h in range(2)]
    peers = ("z", "core", "x", "yh")
    own, other, stat_rows, root_rows, squares = root(
        ids, grad_square, gather_ring(stats), white, part, 2 * col_stats.shape[0],
        lax.axis_size(peers),
    )
    squares = lax.all_to_all(squares, peers, 0, 0, tiled=True)
    update = finish(ids, squares, own, swap(other, "core"))
    return update, exchange_rows(stat_rows, core), exchange_rows(root_rows, core)


def solution(mesh):
    names = ("z", "yl", "core", "x", "yh")
    fine = Mesh(mesh.devices.reshape(8, 2, 2, 4, 2), names)
    row, col = names[:3], names[3:]
    return jax.shard_map(
        shards,
        mesh=fine,
        in_specs=(P(None, col), P(None, row), P(row, None), P(row, col)),
        out_specs=(P(row, col), P(row, col), P(row, col)),
        check_vma=False,
    )
```

```python
import jax
import jax.numpy as jnp
from jax import lax
from jax.sharding import Mesh, PartitionSpec as P
from jax.experimental import pallas as pl
from jax.experimental.pallas import tpu as pltpu

decay_rate = 0.75
damping = 0.001
epsilon = 1e-06
TILE = 256
SLAB = 128
DISTANCES = 5
f32 = jnp.float32
bf16 = jnp.bfloat16


def tdot(a, b):
    return lax.dot_general(a, b, (((0,), (0,)), ((), ())), preferred_element_type=f32)


def dot(a, b):
    return jnp.dot(a, b, preferred_element_type=f32)


def tiles(count, body):
    for j in range(count):
        body(pl.ds(j * TILE, TILE), j)


def slab(ids, k):
    return lax.rem(ids[1] + (1 - 2 * ids[0]) * k + 8, 8)


def front_kernel(ids, acts, g_own, g_other, r_own, r_other, white, gsq, *rest):
    pieces, (grad, wide) = rest[:-2], rest[-2:]
    core = ids[0]
    half = g_own.shape[1]
    size = acts.shape[1]
    slabs = size // SLAB
    gsq[0, 0] = 0.0
    for g, who in ((g_own, core), (g_other, 1 - core)):
        first = pl.multiple_of(who * half, half)

        def fill_grad(cols, j):
            t = tdot(g[...], acts[:, cols]).astype(bf16)
            grad[pl.ds(first, half), cols] = t
            gsq[0, 0] += jnp.sum(jnp.square(t.astype(f32)))

        tiles(size // TILE, fill_grad)
    for r, who in ((r_own, core), (r_other, 1 - core)):
        first = pl.multiple_of(who * half, half)

        def fill_white(cols, j):
            t = dot(r[...], grad[:, cols]).astype(bf16)
            white[pl.ds(first, half), cols] = t
            wide[pl.ds(first, half), cols] = t

        tiles(size // TILE, fill_white)
    wide[:, size:] = white[:, : (DISTANCES - 1) * SLAB]
    for k in range(slabs):
        first = pl.multiple_of(slab(ids, k) * SLAB, SLAB)
        pieces[k][...] = tdot(wide[:, pl.ds(first, SLAB)], wide[:, pl.ds(first, DISTANCES * SLAB)])


def front(ids, acts, g_own, g_other, r_own, r_other):
    tok, half = g_own.shape
    size = r_own.shape[1]
    slabs = size // SLAB
    whole = lambda shape: pl.BlockSpec(
        shape, lambda i, s: (0, 0), pipeline_mode=pl.Buffered(1)
    )
    piece = (SLAB, DISTANCES * SLAB)
    flops = 2 * size * size * (tok + size) + 2 * size * size * DISTANCES * SLAB
    return pl.pallas_call(
        front_kernel,
        out_shape=[
            jax.ShapeDtypeStruct((size, size), bf16),
            jax.ShapeDtypeStruct((1, 1), f32),
        ]
        + [jax.ShapeDtypeStruct(piece, f32)] * slabs,
        grid_spec=pltpu.PrefetchScalarGridSpec(
            num_scalar_prefetch=1,
            grid=(1,),
            in_specs=[
                pl.BlockSpec(
                    (tok, size), lambda i, s: (0, s[0]), pipeline_mode=pl.Buffered(1)
                ),
                whole((tok, half)),
                whole((tok, half)),
                whole((half, size)),
                whole((half, size)),
            ],
            out_specs=[
                whole((size, size)),
                pl.BlockSpec(memory_space=pltpu.SMEM),
            ]
            + [whole(piece)] * slabs,
            scratch_shapes=[
                pltpu.VMEM((size, size), bf16),
                pltpu.VMEM((size, size + (DISTANCES - 1) * SLAB), bf16),
            ],
        ),
        compiler_params=pltpu.CompilerParams(vmem_limit_bytes=24 << 20),
        cost_estimate=pl.CostEstimate(flops=flops, bytes_accessed=12 << 20, transcendentals=0),
        name="front",
    )(ids, acts, g_own, g_other, r_own, r_other)


def halves(x):
    high = x.astype(bf16)
    return high, (x - high.astype(f32)).astype(bf16)


def eye_tile(shape, row, col):
    return (
        lax.broadcasted_iota(jnp.int32, shape, 0) + row
        == lax.broadcasted_iota(jnp.int32, shape, 1) + col
    )


def root_kernel(ids, gsq, *refs):
    slabs = 8
    pieces = refs[:slabs]
    white, part, prod_own, prod_other, stat_rows, root_rows, squares = refs[slabs : slabs + 7]
    y, yh, yl, zh, zl, qh, ql, rh, root = refs[slabs + 7 :]
    core, z, sub = ids[0], ids[1], ids[2]
    size = white.shape[1]
    rows64 = stat_rows.shape[0]
    own = pl.multiple_of(z * SLAB + sub * rows64, rows64)

    def at(k):
        return pl.ds(pl.multiple_of(lax.rem(k, slabs) * SLAB, SLAB), SLAB)

    diagonal = eye_tile((SLAB, SLAB), 0, 0)
    trace = jnp.float32(0)
    for k in range(slabs):
        q = slab(ids, k)
        for d in range(DISTANCES):
            block = pieces[k][:, d * SLAB : (d + 1) * SLAB]
            y[at(q), at(q + d)] = block
            if d == 0:
                trace += jnp.sum(jnp.where(diagonal, block + damping, 0.0))
            elif d < DISTANCES - 1:
                y[at(q + d), at(q)] = block.T
    stat_rows[...] = y[pl.ds(own, rows64), :]
    norm = 2.0 * trace / size
    inverse = 1.0 / norm

    def fill_y(rows, i):
        eye = eye_tile((TILE, size), i * TILE, 0)
        v = (y[rows, :] + jnp.where(eye, damping, 0.0)) * inverse
        y[rows, :] = v
        yh[rows, :], yl[rows, :] = halves(v)

    tiles(size // TILE, fill_y)

    def fill_z(cols, j):
        eye = eye_tile((size, TILE), 0, j * TILE)
        v = dot(yh[...], yh[:, cols]) + (dot(yh[...], yl[:, cols]) + dot(yl[...], yh[:, cols]))
        zh[:, cols], zl[:, cols] = halves(v)
        q = jnp.where(eye, 1.6875, 0.0) - 0.5625 * y[:, cols] + 0.0625 * v
        qh[:, cols], ql[:, cols] = halves(q)

    tiles(size // TILE, fill_z)
    scale = lax.rsqrt(jnp.full((1, 1), norm, f32))

    def fill_root(cols, j):
        eye = eye_tile((size, TILE), 0, j * TILE)
        v = dot(zh[...], qh[:, cols]) + (dot(zh[...], ql[:, cols]) + dot(zl[...], qh[:, cols]))
        v = (jnp.where(eye, 2.25, 0.0) - 2.4375 * y[:, cols] + v) * scale
        root[:, cols] = v
        rh[:, cols] = v.astype(bf16)

    tiles(size // TILE, fill_root)
    root_rows[...] = root[pl.ds(own, rows64), :]
    acc = jnp.zeros((SLAB, size), f32)
    for d in range(DISTANCES):
        weight = 2.0 if 0 < d < DISTANCES - 1 else 1.0
        high, low = halves(part[:, d * SLAB : (d + 1) * SLAB] * weight)
        acc += dot(high, rh[at(z + d), :]) + dot(low, rh[at(z + d), :])
    total = jnp.sum(acc * rh[at(z), :].astype(f32))
    lane = lax.broadcasted_iota(jnp.int32, squares.shape, 2)
    squares[...] = jnp.where(lane == 0, gsq[0, 0], jnp.where(lane == 1, total, 0.0))
    for prod, who in ((prod_own, core), (prod_other, 1 - core)):
        rows = pl.ds(pl.multiple_of(who * (size // 2), size // 2), size // 2)

        def fill_prod(cols, j):
            prod[:, cols] = dot(white[rows, :], rh[:, cols])

        tiles(size // TILE, fill_prod)


def root(ids, gsq, pieces, white, part, rows64, peers):
    size = white.shape[1]
    whole = lambda shape: pl.BlockSpec(
        shape, lambda i, s: (0, 0), pipeline_mode=pl.Buffered(1)
    )
    square = lambda kind: pltpu.VMEM((size, size), kind)
    piece = (SLAB, DISTANCES * SLAB)
    return pl.pallas_call(
        root_kernel,
        out_shape=[
            jax.ShapeDtypeStruct((size // 2, size), f32),
            jax.ShapeDtypeStruct((size // 2, size), f32),
            jax.ShapeDtypeStruct((rows64, size), f32),
            jax.ShapeDtypeStruct((rows64, size), f32),
            jax.ShapeDtypeStruct((peers, 1, 128), f32),
        ],
        grid_spec=pltpu.PrefetchScalarGridSpec(
            num_scalar_prefetch=1,
            grid=(1,),
            in_specs=[pl.BlockSpec(memory_space=pltpu.SMEM)]
            + [whole(piece)] * len(pieces)
            + [whole((size, size)), whole(piece)],
            out_specs=[
                whole((size // 2, size)),
                whole((size // 2, size)),
                whole((rows64, size)),
                whole((rows64, size)),
                pl.BlockSpec((peers, 1, 128), lambda i, s: (0, 0, 0)),
            ],
            scratch_shapes=[square(f32)] + [square(bf16)] * 7 + [square(f32)],
        ),
        compiler_params=pltpu.CompilerParams(vmem_limit_bytes=42 << 20),
        cost_estimate=pl.CostEstimate(
            flops=2 * size**3 * 7, bytes_accessed=12 << 20, transcendentals=0
        ),
        name="root",
    )(ids, gsq, *pieces, white, part)


def finish_kernel(ids, squares, own, other, update):
    size = own.shape[1]
    sums = jnp.sum(squares[...], axis=0)
    scale = jnp.sqrt(sums[:, 0:1] / (sums[:, 1:2] + epsilon))
    for block, who in ((own, ids[0]), (other, 1 - ids[0])):
        cols = pl.ds(pl.multiple_of(who * size, size), size)
        update[:, cols] = (block[...] * scale).astype(update.dtype)


def finish(ids, squares, own, other):
    rows, size = own.shape
    return pl.pallas_call(
        finish_kernel,
        out_shape=jax.ShapeDtypeStruct((rows, 2 * size), bf16),
        grid_spec=pltpu.PrefetchScalarGridSpec(
            num_scalar_prefetch=1,
            grid=(rows // SLAB,),
            in_specs=[
                pl.BlockSpec(squares.shape, lambda i, s: (0, 0, 0)),
                pl.BlockSpec((SLAB, size), lambda i, s: (i, 0)),
                pl.BlockSpec((SLAB, size), lambda i, s: (i, 0)),
            ],
            out_specs=pl.BlockSpec((SLAB, 2 * size), lambda i, s: (i, 0)),
        ),
        compiler_params=pltpu.CompilerParams(vmem_limit_bytes=16 << 20),
        name="finish",
    )(ids, squares, own, other)


def shift(x, by):
    count = lax.axis_size("z")
    route = []
    for z in range(count):
        for core in range(2):
            there = (z + (by if core == 0 else -by)) % count
            route.append((2 * z + core, 2 * there + core))
    return lax.ppermute(x, ("z", "core"), route)


def swap(x, axis):
    return lax.ppermute(x, axis, [(0, 1), (1, 0)])


def by_index(which, mine, other, dim):
    return jnp.where(
        which == 0, jnp.concatenate([mine, other], dim), jnp.concatenate([other, mine], dim)
    )


def gather_stats(col_stats, core, sub, z, size):
    rows = col_stats.shape[0]
    mine = lax.dynamic_slice_in_dim(col_stats, core * size, size, 1)
    theirs = lax.dynamic_slice_in_dim(col_stats, (1 - core) * size, size, 1)
    chip = by_index(core, mine, swap(theirs, "core"), 0)
    wide = jnp.concatenate([chip, chip[:, : (DISTANCES - 1) * SLAB]], 1)
    packed = lax.dynamic_slice(wide, (0, z * SLAB), (2 * rows, DISTANCES * SLAB))
    return by_index(sub, packed, swap(packed, "yl"), 0)


def reduce_ring(pieces):
    up, down = pieces[4], pieces[5]
    for k in range(3):
        up = pieces[3 - k] + shift(up, 1)
        down = shift(down, -1)
        if k < 2:
            down = pieces[6 + k] + down
    return pieces[0] + down + shift(up, 1)


def gather_ring(own):
    pieces = [own] + [None] * 7
    for k in range(4):
        pieces[7 - k] = shift(pieces[-k % 8], 1)
        if k < 3:
            pieces[k + 1] = shift(pieces[k], -1)
    return pieces


def exchange_rows(x, core):
    rows = x.shape[0] // 2
    mine = lax.dynamic_slice_in_dim(x, core * rows, rows, 0)
    theirs = lax.dynamic_slice_in_dim(x, (1 - core) * rows, rows, 0)
    return by_index(core, mine, swap(theirs, "core"), 1)


def shards(acts, grads, row_roots, col_stats):
    size = row_roots.shape[1]
    z, sub, core = lax.axis_index("z"), lax.axis_index("yl"), lax.axis_index("core")
    ids = jnp.stack([core, z, sub]).astype(jnp.int32)
    total_rows = grads.shape[1] * lax.axis_size(("z", "yl", "core"))
    mix = (1.0 - decay_rate) / total_rows

    grads_other, roots_other = swap(grads, "core"), swap(row_roots, "core")
    old = gather_stats(col_stats, core, sub, z, size)
    white, grad_square, *pieces = front(ids, acts, grads, grads_other, row_roots, roots_other)
    grad_square = grad_square + swap(grad_square, "yl")
    part = reduce_ring(pieces)
    part = part + swap(part, "yl")
    stats = decay_rate * old + mix * part
    peers = ("z", "core", "x", "yh")
    own, other, stat_rows, root_rows, squares = root(
        ids, grad_square, gather_ring(stats), white, part, 2 * col_stats.shape[0],
        lax.axis_size(peers),
    )
    squares = lax.all_to_all(squares, peers, 0, 0, tiled=True)
    update = finish(ids, squares, own, swap(other, "core"))
    return update, exchange_rows(stat_rows, core), exchange_rows(root_rows, core)


def solution(mesh):
    names = ("z", "yl", "core", "x", "yh")
    fine = Mesh(mesh.devices.reshape(8, 2, 2, 4, 2), names)
    row, col = names[:3], names[3:]
    return jax.shard_map(
        shards,
        mesh=fine,
        in_specs=(P(None, col), P(None, row), P(row, None), P(row, col)),
        out_specs=(P(row, col), P(row, col), P(row, col)),
        check_vma=False,
    )
```

```python
import jax
import jax.numpy as jnp
from jax import lax
from jax.sharding import Mesh, PartitionSpec as P
from jax.experimental import pallas as pl
from jax.experimental.pallas import tpu as pltpu

decay_rate = 0.75
damping = 0.001
epsilon = 1e-06
TILE = 256
SLAB = 128
DISTANCES = 5
f32 = jnp.float32
bf16 = jnp.bfloat16


def tdot(a, b):
    return lax.dot_general(a, b, (((0,), (0,)), ((), ())), preferred_element_type=f32)


def dot(a, b):
    return jnp.dot(a, b, preferred_element_type=f32)


def tiles(count, body):
    for j in range(count):
        body(pl.ds(j * TILE, TILE), j)


def held(shape, index=None):
    index = index or (lambda i, s: (0,) * len(shape))
    return pl.BlockSpec(shape, index, pipeline_mode=pl.Buffered(1))


def scalar():
    return pl.BlockSpec(memory_space=pltpu.SMEM)


def call(kernel, outs, out_specs, in_specs, scratch, limit, flops, name):
    return pl.pallas_call(
        kernel,
        out_shape=[jax.ShapeDtypeStruct(*o) for o in outs],
        grid_spec=pltpu.PrefetchScalarGridSpec(
            num_scalar_prefetch=1,
            grid=(1,),
            in_specs=in_specs,
            out_specs=out_specs,
            scratch_shapes=scratch,
        ),
        compiler_params=pltpu.CompilerParams(vmem_limit_bytes=limit << 20),
        cost_estimate=pl.CostEstimate(flops=flops, bytes_accessed=8 << 20, transcendentals=0),
        name=name,
    )


def slab(ids, k):
    return lax.rem(ids[1] + k, 8)


def fill_grad(g, acts, grad, first, gsq):
    half = g.shape[1]
    total = jnp.float32(0)
    for j in range(acts.shape[1] // TILE):
        cols = pl.ds(j * TILE, TILE)
        t = tdot(g[...], acts[:, cols]).astype(bf16)
        grad[pl.ds(first, half), cols] = t
        total += jnp.sum(jnp.square(t.astype(f32)))
    gsq[0, 0] = total


def own_grad_kernel(ids, acts, g, grad, gsq):
    fill_grad(g, acts, grad, 0, gsq)


def own_grad(ids, acts, g):
    tok, half = g.shape
    size = acts.shape[1]
    return call(
        own_grad_kernel,
        [((half, size), bf16), ((1, 1), f32)],
        [held((half, size)), scalar()],
        [held((tok, size)), held((tok, half))],
        [],
        12,
        2 * tok * half * size,
        "own_grad",
    )(ids, acts, g)


FIRST = (4, 3, 5, 2, 6, 1, 7, 0)
LATER = ()


def gram(ids, wide, slabs, pieces):
    cut = SLAB // 2
    for i, k in enumerate(slabs):
        first = pl.multiple_of(slab(ids, k) * SLAB, SLAB)
        t = tdot(wide[:, pl.ds(first, SLAB)], wide[:, pl.ds(first, DISTANCES * SLAB)])
        pieces[2 * i][...] = t[:cut]
        pieces[2 * i + 1][...] = t[cut:]


def whiten_kernel(ids, acts, g_other, r_own, r_other, grad_own, wide, gsq, *rest):
    pieces, grad = rest[:-1], rest[-1]
    core = ids[0]
    half = g_other.shape[1]
    size = acts.shape[1]
    fill_grad(grad_own, acts, grad, pl.multiple_of(core * half, half), gsq)
    kept = gsq[0, 0]
    fill_grad(g_other, acts, grad, pl.multiple_of((1 - core) * half, half), gsq)
    gsq[0, 0] += kept
    for r, who in ((r_own, core), (r_other, 1 - core)):
        first = pl.multiple_of(who * half, half)
        for j in range(size // TILE):
            cols = pl.ds(j * TILE, TILE)
            t = dot(r[...], grad[:, cols]).astype(bf16)
            wide[pl.ds(first, half), cols] = t
            if j * TILE < (DISTANCES - 1) * SLAB:
                wide[pl.ds(first, half), pl.ds(size + j * TILE, TILE)] = t
    gram(ids, wide, FIRST, pieces)


PIECE = (SLAB // 2, DISTANCES * SLAB)


def whiten(ids, acts, g_other, r_own, r_other, grad_own):
    tok, half = g_other.shape
    size = acts.shape[1]
    wide = (size, size + (DISTANCES - 1) * SLAB)
    return call(
        whiten_kernel,
        [(wide, bf16), ((1, 1), f32)] + [(PIECE, f32)] * 2 * len(FIRST),
        [held(wide), scalar()] + [held(PIECE)] * 2 * len(FIRST),
        [held((tok, size)), held((tok, half)), held((half, size)), held((half, size)), held((tok, half))],
        [pltpu.VMEM((size, size), bf16)],
        24,
        2 * size * size * (half + size),
        "whiten",
    )(ids, acts, g_other, r_own, r_other, grad_own)


def later_gram_kernel(ids, wide, *pieces):
    gram(ids, wide, LATER, pieces)


def later_gram(ids, wide):
    return call(
        later_gram_kernel,
        [(PIECE, f32)] * 2 * len(LATER),
        [held(PIECE)] * 2 * len(LATER),
        [held(wide.shape)],
        [],
        16,
        2 * wide.shape[0] * SLAB * DISTANCES * SLAB * len(LATER),
        "later_gram",
    )(ids, wide)


def halves(x):
    high = x.astype(bf16)
    return high, (x - high.astype(f32)).astype(bf16)


def eye_tile(shape, row, col):
    return (
        lax.broadcasted_iota(jnp.int32, shape, 0) + row
        == lax.broadcasted_iota(jnp.int32, shape, 1) + col
    )


def root_kernel(ids, gsq_own, gsq_other, *refs):
    slabs = 8
    pieces = refs[: 2 * slabs]
    part_a, part_b, rh, stat_rows, root_rows, squares = refs[2 * slabs : 2 * slabs + 6]
    y, yh, yl, zh, zl, qh, ql, root = refs[2 * slabs + 6 :]
    z, sub = ids[1], ids[2]
    size = rh.shape[1]
    cut = SLAB // 2
    rows64 = stat_rows.shape[0]
    own = pl.multiple_of(z * SLAB + sub * rows64, rows64)

    def at(k):
        return pl.ds(pl.multiple_of(lax.rem(k, slabs) * SLAB, SLAB), SLAB)

    diagonal = eye_tile((SLAB, SLAB), 0, 0)
    trace = jnp.float32(0)
    for k in range(slabs):
        q = slab(ids, k)
        for d in range(DISTANCES):
            cols = slice(d * SLAB, (d + 1) * SLAB)
            block = jnp.concatenate([pieces[2 * k][:, cols], pieces[2 * k + 1][:, cols]], 0)
            y[at(q), at(q + d)] = block
            if d == 0:
                trace += jnp.sum(jnp.where(diagonal, block + damping, 0.0))
            elif d < DISTANCES - 1:
                y[at(q + d), at(q)] = block.T
    stat_rows[...] = y[pl.ds(own, rows64), :]
    norm = 2.0 * trace / size
    inverse = 1.0 / norm

    def fill_y(rows, i):
        eye = eye_tile((TILE, size), i * TILE, 0)
        v = (y[rows, :] + jnp.where(eye, damping, 0.0)) * inverse
        y[rows, :] = v
        yh[rows, :], yl[rows, :] = halves(v)

    tiles(size // TILE, fill_y)

    def fill_z(cols, j):
        eye = eye_tile((size, TILE), 0, j * TILE)
        v = dot(yh[...], yh[:, cols]) + (dot(yh[...], yl[:, cols]) + dot(yl[...], yh[:, cols]))
        zh[:, cols], zl[:, cols] = halves(v)
        q = jnp.where(eye, 1.6875, 0.0) - 0.5625 * y[:, cols] + 0.0625 * v
        qh[:, cols], ql[:, cols] = halves(q)

    tiles(size // TILE, fill_z)
    scale = lax.rsqrt(jnp.full((1, 1), norm, f32))

    def fill_root(cols, j):
        eye = eye_tile((size, TILE), 0, j * TILE)
        v = dot(zh[...], qh[:, cols]) + (dot(zh[...], ql[:, cols]) + dot(zl[...], qh[:, cols]))
        v = (jnp.where(eye, 2.25, 0.0) - 2.4375 * y[:, cols] + v) * scale
        root[:, cols] = v
        rh[:, cols] = v.astype(bf16)

    tiles(size // TILE, fill_root)
    root_rows[...] = root[pl.ds(own, rows64), :]
    acc = jnp.zeros((SLAB, size), f32)
    for d in range(DISTANCES):
        cols = slice(d * SLAB, (d + 1) * SLAB)
        weight = 2.0 if 0 < d < DISTANCES - 1 else 1.0
        high, low = halves(jnp.concatenate([part_a[:, cols], part_b[:, cols]], 0) * weight)
        acc += dot(high, rh[at(z + d), :]) + dot(low, rh[at(z + d), :])
    total = jnp.sum(acc * rh[at(z), :].astype(f32))
    lane = lax.broadcasted_iota(jnp.int32, squares.shape, 2)
    squares[...] = jnp.where(
        lane == 0, gsq_own[0, 0] + gsq_other[0, 0], jnp.where(lane == 1, total, 0.0)
    )


def root(ids, gsq_own, gsq_other, pieces, part, size, rows64, peers):
    square = lambda kind: pltpu.VMEM((size, size), kind)
    return call(
        root_kernel,
        [
            ((size, size), bf16),
            ((rows64, size), f32),
            ((rows64, size), f32),
            ((peers, 1, 128), f32),
        ],
        [held((size, size)), held((rows64, size)), held((rows64, size)), held((peers, 1, 128))],
        [scalar(), scalar()] + [held(PIECE)] * (len(pieces) + 2),
        [square(f32)] + [square(bf16)] * 6 + [square(f32)],
        40,
        2 * size**3 * 6,
        "root",
    )(ids, gsq_own, gsq_other, *pieces, *part)


def product_kernel(ids, wide, rh, own, other):
    size = rh.shape[0]
    half = size // 2
    for out, who in ((own, ids[0]), (other, 1 - ids[0])):
        rows = pl.ds(pl.multiple_of(who * half, half), half)
        for j in range(size // TILE):
            cols = pl.ds(j * TILE, TILE)
            out[:, cols] = dot(wide[rows, :size], rh[:, cols])


def product(ids, wide, rh):
    size = rh.shape[0]
    return call(
        product_kernel,
        [((size // 2, size), f32)] * 2,
        [held((size // 2, size))] * 2,
        [held(wide.shape), held(rh.shape)],
        [],
        16,
        2 * size**3,
        "product",
    )(ids, wide, rh)


def finish_kernel(ids, squares, own, other, update, kept):
    size = own.shape[1]

    @pl.when(pl.program_id(0) == 0)
    def _():
        sums = jnp.sum(squares[...], axis=0)
        kept[...] = jnp.broadcast_to(
            jnp.sqrt(sums[:, 0:1] / (sums[:, 1:2] + epsilon)), kept.shape
        )

    scale = kept[0:1, 0:1]
    for block, who in ((own, ids[0]), (other, 1 - ids[0])):
        cols = pl.ds(pl.multiple_of(who * size, size), size)
        update[:, cols] = (block[...] * scale).astype(update.dtype)


def finish(ids, squares, own, other):
    rows, size = own.shape
    return pl.pallas_call(
        finish_kernel,
        out_shape=jax.ShapeDtypeStruct((rows, 2 * size), bf16),
        grid_spec=pltpu.PrefetchScalarGridSpec(
            num_scalar_prefetch=1,
            grid=(rows // SLAB,),
            in_specs=[
                pl.BlockSpec(squares.shape, lambda i, s: (0, 0, 0)),
                pl.BlockSpec((SLAB, size), lambda i, s: (i, 0)),
                pl.BlockSpec((SLAB, size), lambda i, s: (i, 0)),
            ],
            out_specs=pl.BlockSpec((SLAB, 2 * size), lambda i, s: (i, 0)),
            scratch_shapes=[pltpu.VMEM((8, 128), f32)],
        ),
        compiler_params=pltpu.CompilerParams(vmem_limit_bytes=16 << 20),
        name="finish",
    )(ids, squares, own, other)


def shift(x, by):
    count = lax.axis_size("z")
    return lax.ppermute(x, "z", [(i, (i + by) % count) for i in range(count)])


def swap(x, axis):
    return lax.ppermute(x, axis, [(0, 1), (1, 0)])


def by_index(which, mine, other, dim):
    return jnp.where(
        which == 0, jnp.concatenate([mine, other], dim), jnp.concatenate([other, mine], dim)
    )


def gather_stats(col_stats, core, sub, z, size):
    rows = col_stats.shape[0]
    mine = lax.dynamic_slice_in_dim(col_stats, core * size, size, 1)
    theirs = lax.dynamic_slice_in_dim(col_stats, (1 - core) * size, size, 1)
    chip = by_index(core, mine, swap(theirs, "core"), 0)
    wide = jnp.concatenate([chip, chip[:, : (DISTANCES - 1) * SLAB]], 1)
    packed = lax.dynamic_slice(wide, (0, z * SLAB), (2 * rows, DISTANCES * SLAB))
    return by_index(sub, packed, swap(packed, "yl"), 0)


def reduce_ring(pieces):
    def chain(h, first, by):
        sum_ = shift(pieces[2 * first + h], by)
        for k in range(first - by, 0 if by > 0 else 8, -by):
            sum_ = shift(pieces[2 * k + h] + sum_, by)
        return sum_

    up_a, down_b = chain(0, 4, 1), chain(1, 4, -1)
    up_b, down_a = chain(1, 3, 1), chain(0, 5, -1)
    return pieces[0] + up_a + down_a, pieces[1] + up_b + down_b


def gather_ring(own):
    pieces = list(own) + [None] * 14
    for hops in range(4):
        for h, by in ((0, 1), (1, -1), (1, 1), (0, -1)):
            if hops == 3 and (h, by) in ((1, 1), (0, -1)):
                continue
            source = -by * hops % 8
            pieces[2 * (-by * (hops + 1) % 8) + h] = shift(pieces[2 * source + h], by)
    return pieces


def exchange_rows(x, core):
    rows = x.shape[0] // 2
    mine = lax.dynamic_slice_in_dim(x, core * rows, rows, 0)
    theirs = lax.dynamic_slice_in_dim(x, (1 - core) * rows, rows, 0)
    return by_index(core, mine, swap(theirs, "core"), 1)


def shards(acts, grads, row_roots, col_stats):
    size = row_roots.shape[1]
    z, sub, core = lax.axis_index("z"), lax.axis_index("yl"), lax.axis_index("core")
    ids = jnp.stack([core, z, sub]).astype(jnp.int32)
    total_rows = grads.shape[1] * lax.axis_size(("z", "yl", "core"))
    mix = (1.0 - decay_rate) / total_rows

    grads_other, roots_other = swap(grads, "core"), swap(row_roots, "core")
    mine = lax.dynamic_slice_in_dim(acts, core * size, size, 1)
    old = gather_stats(col_stats, core, sub, z, size)
    wide, gsq_other, *first = whiten(ids, mine, grads_other, row_roots, roots_other, grads)
    later = ()
    pieces = [None] * 16
    for i, k in enumerate(FIRST):
        pieces[2 * k : 2 * k + 2] = first[2 * i : 2 * i + 2]
    for i, k in enumerate(LATER):
        pieces[2 * k : 2 * k + 2] = later[2 * i : 2 * i + 2]
    gsq = gsq_other
    part = [p + swap(p, "yl") for p in reduce_ring(pieces)]
    cut = SLAB // 2
    stats = [decay_rate * old[h * cut : (h + 1) * cut] + mix * part[h] for h in range(2)]
    peers = ("z", "core", "x", "yh")
    half_roots, stat_rows, root_rows, squares = root(
        ids, gsq, swap(gsq, "yl"), gather_ring(stats), part, size, 2 * col_stats.shape[0],
        lax.axis_size(peers),
    )
    squares = lax.all_to_all(squares, peers, 0, 0, tiled=True)
    own, other = product(ids, wide, half_roots)
    update = finish(ids, squares, own, swap(other, "core"))
    return update, exchange_rows(stat_rows, core), exchange_rows(root_rows, core)


def solution(mesh):
    names = ("z", "yl", "core", "x", "yh")
    fine = Mesh(mesh.devices.reshape(8, 2, 2, 4, 2), names)
    row, col = names[:3], names[3:]
    return jax.shard_map(
        shards,
        mesh=fine,
        in_specs=(P(None, col), P(None, row), P(row, None), P(row, col)),
        out_specs=(P(row, col), P(row, col), P(row, col)),
        check_vma=False,
    )
```

```python
import jax
import jax.numpy as jnp
from jax import lax
from jax.sharding import Mesh, PartitionSpec as P
from jax.experimental import pallas as pl
from jax.experimental.pallas import tpu as pltpu

decay_rate = 0.75
damping = 0.001
epsilon = 1e-06
TILE = 256
SLAB = 128
DISTANCES = 5
f32 = jnp.float32
bf16 = jnp.bfloat16


def tdot(a, b):
    return lax.dot_general(a, b, (((0,), (0,)), ((), ())), preferred_element_type=f32)


def dot(a, b):
    return jnp.dot(a, b, preferred_element_type=f32)


def tiles(count, body):
    def turn(j, carry):
        body(pl.ds(pl.multiple_of(j * TILE, TILE), TILE), j)
        return carry

    lax.fori_loop(0, count, turn, 0)


def for_halves(body, half):
    def turn(i, carry):
        body(pl.ds(pl.multiple_of(i * half, half), half), i)
        return carry

    lax.fori_loop(0, 2, turn, 0)


def held(shape, index=None):
    index = index or (lambda i, s: (0,) * len(shape))
    return pl.BlockSpec(shape, index, pipeline_mode=pl.Buffered(1))


def scalar():
    return pl.BlockSpec(memory_space=pltpu.SMEM)


def call(kernel, outs, out_specs, in_specs, scratch, limit, flops, name):
    return pl.pallas_call(
        kernel,
        out_shape=[jax.ShapeDtypeStruct(*o) for o in outs],
        grid_spec=pltpu.PrefetchScalarGridSpec(
            num_scalar_prefetch=1,
            grid=(1,),
            in_specs=in_specs,
            out_specs=out_specs,
            scratch_shapes=scratch,
        ),
        compiler_params=pltpu.CompilerParams(vmem_limit_bytes=limit << 20),
        cost_estimate=pl.CostEstimate(flops=flops, bytes_accessed=8 << 20, transcendentals=0),
        name=name,
    )


def slab(ids, k):
    return lax.rem(ids[1] + k, 8)


def fill_grad(g, acts, grad, first, gsq):
    half = g.shape[1]

    def fill(cols, j):
        t = tdot(g[...], acts[:, cols]).astype(bf16)
        grad[pl.ds(first, half), cols] = t
        gsq[0, 0] += jnp.sum(jnp.square(t.astype(f32)))

    tiles(acts.shape[1] // TILE, fill)


def whiten_kernel(ids, acts, g_own, g_other, r_own, r_other, wide, gsq, *rest):
    pieces, grad = rest[:-1], rest[-1]
    core = ids[0]
    half = g_own.shape[1]
    size = acts.shape[1]
    cut = SLAB // 2
    gsq[0, 0] = 0.0
    for g, who in ((g_own, core), (g_other, 1 - core)):
        fill_grad(g, acts, grad, pl.multiple_of(who * half, half), gsq)
    for r, who in ((r_own, core), (r_other, 1 - core)):
        first = pl.multiple_of(who * half, half)

        def fill_white(cols, j):
            wide[pl.ds(first, half), cols] = dot(r[...], grad[:, cols]).astype(bf16)

        tiles(size // TILE, fill_white)
    wide[:, size:] = wide[:, : (DISTANCES - 1) * SLAB]
    for k in range(size // SLAB):
        first = pl.multiple_of(slab(ids, k) * SLAB, SLAB)
        t = tdot(wide[:, pl.ds(first, SLAB)], wide[:, pl.ds(first, DISTANCES * SLAB)])
        pieces[2 * k][...] = t[:cut]
        pieces[2 * k + 1][...] = t[cut:]


WHITEN_MIB = 48
PIECE = (SLAB // 2, DISTANCES * SLAB)


def whiten(ids, acts, g_own, g_other, r_own, r_other):
    tok, half = g_own.shape
    size = acts.shape[1]
    count = 2 * size // SLAB
    wide = (size, size + (DISTANCES - 1) * SLAB)
    return call(
        whiten_kernel,
        [(wide, bf16), ((1, 1), f32)] + [(PIECE, f32)] * count,
        [held(wide), scalar()] + [held(PIECE)] * count,
        [held((tok, size))] + [held((tok, half))] * 2 + [held((half, size))] * 2,
        [pltpu.VMEM((size, size), bf16)],
        WHITEN_MIB,
        2 * size * size * (tok + size + DISTANCES * SLAB),
        "whiten",
    )(ids, acts, g_own, g_other, r_own, r_other)


def halves(x):
    high = x.astype(bf16)
    return high, (x - high.astype(f32)).astype(bf16)


def eye_tile(shape, row, col):
    return (
        lax.broadcasted_iota(jnp.int32, shape, 0) + row
        == lax.broadcasted_iota(jnp.int32, shape, 1) + col
    )


def root_kernel(ids, gsq, *refs):
    slabs = 8
    pieces = refs[: 2 * slabs]
    part_a, part_b, rh, kept_rows, squares = refs[2 * slabs : 2 * slabs + 5]
    y, yh, yl, zh, zl, qh, ql, root = refs[2 * slabs + 5 :]
    z, sub = ids[1], ids[2]
    size = rh.shape[1]
    cut = SLAB // 2
    quarter = kept_rows.shape[0] // 4

    def keep(source, place):
        for core in range(2):
            first = z * SLAB + (2 * sub + core) * quarter
            kept_rows[pl.ds((2 * core + place) * quarter, quarter), :] = source[
                pl.ds(pl.multiple_of(first, quarter), quarter), :
            ]


    def at(k):
        return pl.ds(pl.multiple_of(lax.rem(k, slabs) * SLAB, SLAB), SLAB)

    diagonal = eye_tile((SLAB, SLAB), 0, 0)
    trace = jnp.float32(0)
    for k in range(slabs):
        q = slab(ids, k)
        for d in range(DISTANCES):
            cols = slice(d * SLAB, (d + 1) * SLAB)
            block = jnp.concatenate([pieces[2 * k][:, cols], pieces[2 * k + 1][:, cols]], 0)
            y[at(q), at(q + d)] = block
            if d == 0:
                trace += jnp.sum(jnp.where(diagonal, block + damping, 0.0))
            elif d < DISTANCES - 1:
                y[at(q + d), at(q)] = block.T
    keep(y, 0)
    norm = 2.0 * trace / size
    inverse = 1.0 / norm

    def fill_y(rows, i):
        eye = eye_tile((TILE, size), i * TILE, 0)
        v = (y[rows, :] + jnp.where(eye, damping, 0.0)) * inverse
        y[rows, :] = v
        yh[rows, :], yl[rows, :] = halves(v)

    tiles(size // TILE, fill_y)

    half = size // 2

    def fill_z(cols, j):
        for_halves(lambda rows, i: fill_z_half(rows, cols, i, j), half)

    def fill_z_half(rows, cols, i, j):
        eye = eye_tile((half, TILE), i * half, j * TILE)
        v = dot(yh[rows, :], yh[:, cols]) + (
            dot(yh[rows, :], yl[:, cols]) + dot(yl[rows, :], yh[:, cols])
        )
        zh[rows, cols], zl[rows, cols] = halves(v)
        q = jnp.where(eye, 1.6875, 0.0) - 0.5625 * y[rows, cols] + 0.0625 * v
        qh[rows, cols], ql[rows, cols] = halves(q)

    tiles(size // TILE, fill_z)
    scale = lax.rsqrt(jnp.full((1, 1), norm, f32))

    def fill_root(cols, j):
        for_halves(lambda rows, i: fill_root_half(rows, cols, i, j), half)

    def fill_root_half(rows, cols, i, j):
        eye = eye_tile((half, TILE), i * half, j * TILE)
        v = dot(zh[rows, :], qh[:, cols]) + (
            dot(zh[rows, :], ql[:, cols]) + dot(zl[rows, :], qh[:, cols])
        )
        v = (jnp.where(eye, 2.25, 0.0) - 2.4375 * y[rows, cols] + v) * scale
        root[rows, cols] = v
        rh[rows, cols] = v.astype(bf16)

    tiles(size // TILE, fill_root)
    keep(root, 1)
    acc = jnp.zeros((SLAB, size), f32)
    for d in range(DISTANCES):
        cols = slice(d * SLAB, (d + 1) * SLAB)
        weight = 2.0 if 0 < d < DISTANCES - 1 else 1.0
        high, low = halves(jnp.concatenate([part_a[:, cols], part_b[:, cols]], 0) * weight)
        acc += dot(high, rh[at(z + d), :]) + dot(low, rh[at(z + d), :])
    total = jnp.sum(acc * rh[at(z), :].astype(f32))
    lane = lax.broadcasted_iota(jnp.int32, squares.shape, 2)
    squares[...] = jnp.where(lane == 0, gsq[0, 0], jnp.where(lane == 1, total, 0.0))


def root(ids, gsq, pieces, part, size, rows, peers):
    square = lambda kind: pltpu.VMEM((size, size), kind)
    return call(
        root_kernel,
        [((size, size), bf16), ((rows, size), f32), ((peers, 1, 128), f32)],
        [held((size, size)), held((rows, size)), held((peers, 1, 128))],
        [scalar()] + [held(PIECE)] * (len(pieces) + 2),
        [square(f32)] + [square(bf16)] * 6 + [square(f32)],
        40,
        2 * size**3 * 6,
        "root",
    )(ids, gsq, *pieces, *part)


def product_kernel(ids, wide, rh, own, other):
    size = rh.shape[0]
    half = size // 2
    for out, who in ((own, ids[0]), (other, 1 - ids[0])):
        rows = pl.ds(pl.multiple_of(who * half, half), half)

        def fill(cols, j):
            out[:, cols] = dot(wide[rows, :size], rh[:, cols])

        tiles(size // TILE, fill)


def product(ids, wide, rh):
    size = rh.shape[0]
    return call(
        product_kernel,
        [((size // 2, size), f32)] * 2,
        [held((size // 2, size))] * 2,
        [held(wide.shape), held(rh.shape)],
        [],
        16,
        2 * size**3,
        "product",
    )(ids, wide, rh)


def finish_kernel(ids, squares, own, other, update, kept):
    size = own.shape[1]

    @pl.when(pl.program_id(0) == 0)
    def _():
        sums = jnp.sum(squares[...], axis=0)
        kept[...] = jnp.broadcast_to(
            jnp.sqrt(sums[:, 0:1] / (sums[:, 1:2] + epsilon)), kept.shape
        )

    scale = kept[0:1, 0:1]
    for block, who in ((own, ids[0]), (other, 1 - ids[0])):
        cols = pl.ds(pl.multiple_of(who * size, size), size)
        update[:, cols] = (block[...] * scale).astype(update.dtype)


def finish(ids, squares, own, other):
    rows, size = own.shape
    return pl.pallas_call(
        finish_kernel,
        out_shape=jax.ShapeDtypeStruct((rows, 2 * size), bf16),
        grid_spec=pltpu.PrefetchScalarGridSpec(
            num_scalar_prefetch=1,
            grid=(rows // SLAB,),
            in_specs=[
                pl.BlockSpec(squares.shape, lambda i, s: (0, 0, 0)),
                pl.BlockSpec((SLAB, size), lambda i, s: (i, 0)),
                pl.BlockSpec((SLAB, size), lambda i, s: (i, 0)),
            ],
            out_specs=pl.BlockSpec((SLAB, 2 * size), lambda i, s: (i, 0)),
            scratch_shapes=[pltpu.VMEM((8, 128), f32)],
        ),
        compiler_params=pltpu.CompilerParams(vmem_limit_bytes=16 << 20),
        name="finish",
    )(ids, squares, own, other)


def shift(x, by):
    count = lax.axis_size("z")
    return lax.ppermute(x, "z", [(i, (i + by) % count) for i in range(count)])


def swap(x, axis):
    return lax.ppermute(x, axis, [(0, 1), (1, 0)])


def by_index(which, mine, other, dim):
    return jnp.where(
        which == 0, jnp.concatenate([mine, other], dim), jnp.concatenate([other, mine], dim)
    )


def chip_stats(col_stats, core, z, size):
    rows = col_stats.shape[0]
    mine = lax.dynamic_slice_in_dim(col_stats, core * size, size, 1)
    theirs = lax.dynamic_slice_in_dim(col_stats, (1 - core) * size, size, 1)
    chip = by_index(core, mine, swap(theirs, "core"), 0)
    wide = jnp.concatenate([chip, chip[:, : (DISTANCES - 1) * SLAB]], 1)
    return lax.dynamic_slice(wide, (0, z * SLAB), (2 * rows, DISTANCES * SLAB))


def reduce_ring(pieces):
    def chain(h, first, by):
        sum_ = shift(pieces[2 * first + h], by)
        for k in range(first - by, 0 if by > 0 else 8, -by):
            sum_ = shift(pieces[2 * k + h] + sum_, by)
        return sum_

    up_a, down_b = chain(0, 4, 1), chain(1, 4, -1)
    up_b, down_a = chain(1, 3, 1), chain(0, 5, -1)
    return pieces[0] + up_a + down_a, pieces[1] + up_b + down_b


def gather_ring(own):
    pieces = list(own) + [None] * 14
    for hops in range(4):
        for h, by in ((0, 1), (1, -1), (1, 1), (0, -1)):
            if hops == 3 and (h, by) in ((1, 1), (0, -1)):
                continue
            source = -by * hops % 8
            pieces[2 * (-by * (hops + 1) % 8) + h] = shift(pieces[2 * source + h], by)
    return pieces


def exchange_rows(x, core):
    rows = x.shape[0] // 2
    mine = lax.dynamic_slice_in_dim(x, core * rows, rows, 0)
    theirs = lax.dynamic_slice_in_dim(x, (1 - core) * rows, rows, 0)
    return by_index(core, mine, swap(theirs, "core"), 1)


def shards(acts, grads, row_roots, col_stats):
    size = row_roots.shape[1]
    z, sub, core = lax.axis_index("z"), lax.axis_index("yl"), lax.axis_index("core")
    ids = jnp.stack([core, z, sub]).astype(jnp.int32)
    total_rows = grads.shape[1] * lax.axis_size(("z", "yl", "core"))
    mix = (1.0 - decay_rate) / total_rows

    grads_other, roots_other = swap(grads, "core"), swap(row_roots, "core")
    mine = lax.dynamic_slice_in_dim(acts, core * size, size, 1)
    old = decay_rate * chip_stats(col_stats, core, z, size)
    wide, gsq, *pieces = whiten(ids, mine, grads, grads_other, row_roots, roots_other)
    part = reduce_ring(pieces)
    stats = [mix * part[h] + jnp.where(sub == h, old, 0.0) for h in range(2)]
    stats = [x + swap(x, "yl") for x in stats]
    peers = ("z", "yl", "core", "x", "yh")
    rows = col_stats.shape[0]
    half_roots, kept_rows, squares = root(
        ids, gsq, gather_ring(stats), part, size, 4 * rows, lax.axis_size(peers)
    )
    squares = lax.all_to_all(squares, peers, 0, 0, tiled=True)
    own, other = product(ids, wide, half_roots)
    update = finish(ids, squares, own, swap(other, "core"))
    kept_rows = exchange_rows(kept_rows, core)
    return update, kept_rows[:rows], kept_rows[rows:]


def solution(mesh):
    names = ("z", "yl", "core", "x", "yh")
    fine = Mesh(mesh.devices.reshape(8, 2, 2, 4, 2), names)
    row, col = names[:3], names[3:]
    return jax.shard_map(
        shards,
        mesh=fine,
        in_specs=(P(None, col), P(None, row), P(row, None), P(row, col)),
        out_specs=(P(row, col), P(row, col), P(row, col)),
        check_vma=False,
    )
```

```python
import jax
import jax.numpy as jnp
from jax import lax
from jax.sharding import Mesh, PartitionSpec as P
from jax.experimental import pallas as pl
from jax.experimental.pallas import tpu as pltpu

decay_rate = 0.75
damping = 0.001
epsilon = 1e-06
TILE = 256
SLAB = 128
DISTANCES = 5
f32 = jnp.float32
bf16 = jnp.bfloat16


def tdot(a, b):
    return lax.dot_general(a, b, (((0,), (0,)), ((), ())), preferred_element_type=f32)


def dot(a, b):
    return jnp.dot(a, b, preferred_element_type=f32)


def tiles(count, body):
    def turn(j, carry):
        body(pl.ds(pl.multiple_of(j * TILE, TILE), TILE), j)
        return carry

    lax.fori_loop(0, count, turn, 0)


def for_halves(body, half):
    def turn(i, carry):
        body(pl.ds(pl.multiple_of(i * half, half), half), i)
        return carry

    lax.fori_loop(0, 2, turn, 0)


def held(shape, index=None):
    index = index or (lambda i, s: (0,) * len(shape))
    return pl.BlockSpec(shape, index, pipeline_mode=pl.Buffered(1))


def scalar():
    return pl.BlockSpec(memory_space=pltpu.SMEM)


def call(kernel, outs, out_specs, in_specs, scratch, limit, flops, name):
    return pl.pallas_call(
        kernel,
        out_shape=[jax.ShapeDtypeStruct(*o) for o in outs],
        grid_spec=pltpu.PrefetchScalarGridSpec(
            num_scalar_prefetch=1,
            grid=(1,),
            in_specs=in_specs,
            out_specs=out_specs,
            scratch_shapes=scratch,
        ),
        compiler_params=pltpu.CompilerParams(vmem_limit_bytes=limit << 20),
        cost_estimate=pl.CostEstimate(flops=flops, bytes_accessed=8 << 20, transcendentals=0),
        name=name,
    )


def slab(ids, k):
    return lax.rem(ids[1] + k, 8)


def whiten_kernel(ids, acts, g_own, g_other, r_own, r_other, wide, gsq, *rest):
    pieces, (block, g, r, grad, tile_sems, sems) = rest[:-6], rest[-6:]
    core = ids[0]
    half = g_own.shape[1]
    size = block.shape[1]
    cut = SLAB // 2

    def tile_copy(j):
        source = pl.ds(pl.multiple_of(core * size + j * TILE, TILE), TILE)
        target = pl.ds(pl.multiple_of(j * TILE, TILE), TILE)
        return pltpu.make_async_copy(acts.at[:, source], block.at[:, target], tile_sems.at[j])

    copies = [
        pltpu.make_async_copy(source, target, sems.at[i])
        for i, (source, target) in enumerate(
            ((g_own, g.at[0]), (g_other, g.at[1]), (r_own, r.at[0]), (r_other, r.at[1]))
        )
    ]
    copies[0].start()
    for j in range(size // TILE):
        tile_copy(j).start()
    for copy in copies[1:]:
        copy.start()
    gsq[0, 0] = 0.0
    for i, who in enumerate((core, 1 - core)):
        first = pl.multiple_of(who * half, half)
        copies[i].wait()

        def fill_grad(cols, j):
            if i == 0:
                tile_copy(j).wait()
            t = tdot(g[i], block[:, cols]).astype(bf16)
            grad[pl.ds(first, half), cols] = t
            gsq[0, 0] += jnp.sum(jnp.square(t.astype(f32)))

        tiles(size // TILE, fill_grad)
    for i, who in enumerate((core, 1 - core)):
        first = pl.multiple_of(who * half, half)
        copies[2 + i].wait()

        def fill_white(cols, j):
            wide[pl.ds(first, half), cols] = dot(r[i], grad[:, cols]).astype(bf16)

        tiles(size // TILE, fill_white)
    wide[:, size:] = wide[:, : (DISTANCES - 1) * SLAB]
    for k in range(size // SLAB):
        first = pl.multiple_of(slab(ids, k) * SLAB, SLAB)
        t = tdot(wide[:, pl.ds(first, SLAB)], wide[:, pl.ds(first, DISTANCES * SLAB)])
        pieces[2 * k][...] = t[:cut]
        pieces[2 * k + 1][...] = t[cut:]


WHITEN_MIB = 52
PIECE = (SLAB // 2, DISTANCES * SLAB)


def whiten(ids, acts, g_own, g_other, r_own, r_other):
    tok, half = g_own.shape
    size = r_own.shape[1]
    count = 2 * size // SLAB
    wide = (size, size + (DISTANCES - 1) * SLAB)
    return call(
        whiten_kernel,
        [(wide, bf16), ((1, 1), f32)] + [(PIECE, f32)] * count,
        [held(wide), scalar()] + [held(PIECE)] * count,
        [pl.BlockSpec(memory_space=pl.ANY)] * 5,
        [
            pltpu.VMEM((tok, size), bf16),
            pltpu.VMEM((2, tok, half), bf16),
            pltpu.VMEM((2, half, size), bf16),
            pltpu.VMEM((size, size), bf16),
            pltpu.SemaphoreType.DMA((size // TILE,)),
            pltpu.SemaphoreType.DMA((4,)),
        ],
        WHITEN_MIB,
        2 * size * size * (tok + size + DISTANCES * SLAB),
        "whiten",
    )(ids, acts, g_own, g_other, r_own, r_other)


def halves(x):
    high = x.astype(bf16)
    return high, (x - high.astype(f32)).astype(bf16)


def eye_tile(shape, row, col):
    return (
        lax.broadcasted_iota(jnp.int32, shape, 0) + row
        == lax.broadcasted_iota(jnp.int32, shape, 1) + col
    )


def root_kernel(ids, gsq, *refs):
    slabs = 8
    pieces = refs[: 2 * slabs]
    part_a, part_b, wide, own, other, kept_rows, squares = refs[2 * slabs : 2 * slabs + 7]
    y, yh, yl, zh, zl, qh, ql, rh, root, white, white_sem = refs[2 * slabs + 7 :]
    white_copy = pltpu.make_async_copy(wide.at[:, pl.ds(0, rh.shape[1])], white, white_sem.at[0])
    white_copy.start()
    z, sub = ids[1], ids[2]
    size = rh.shape[1]
    cut = SLAB // 2
    quarter = kept_rows.shape[0] // 4

    def keep(source, place):
        for core in range(2):
            first = z * SLAB + (2 * sub + core) * quarter
            kept_rows[pl.ds((2 * core + place) * quarter, quarter), :] = source[
                pl.ds(pl.multiple_of(first, quarter), quarter), :
            ]


    def at(k):
        return pl.ds(pl.multiple_of(lax.rem(k, slabs) * SLAB, SLAB), SLAB)

    diagonal = eye_tile((SLAB, SLAB), 0, 0)
    trace = jnp.float32(0)
    for k in range(slabs):
        q = slab(ids, k)
        for d in range(DISTANCES):
            cols = slice(d * SLAB, (d + 1) * SLAB)
            block = jnp.concatenate([pieces[2 * k][:, cols], pieces[2 * k + 1][:, cols]], 0)
            y[at(q), at(q + d)] = block
            if d == 0:
                trace += jnp.sum(jnp.where(diagonal, block + damping, 0.0))
            elif d < DISTANCES - 1:
                y[at(q + d), at(q)] = block.T
    keep(y, 0)
    norm = 2.0 * trace / size
    inverse = 1.0 / norm

    def fill_y(rows, i):
        eye = eye_tile((TILE, size), i * TILE, 0)
        v = (y[rows, :] + jnp.where(eye, damping, 0.0)) * inverse
        y[rows, :] = v
        yh[rows, :], yl[rows, :] = halves(v)

    tiles(size // TILE, fill_y)

    half = size // 2

    def fill_z(cols, j):
        for_halves(lambda rows, i: fill_z_half(rows, cols, i, j), half)

    def fill_z_half(rows, cols, i, j):
        eye = eye_tile((half, TILE), i * half, j * TILE)
        v = dot(yh[rows, :], yh[:, cols]) + (
            dot(yh[rows, :], yl[:, cols]) + dot(yl[rows, :], yh[:, cols])
        )
        zh[rows, cols], zl[rows, cols] = halves(v)
        q = jnp.where(eye, 1.6875, 0.0) - 0.5625 * y[rows, cols] + 0.0625 * v
        qh[rows, cols], ql[rows, cols] = halves(q)

    tiles(size // TILE, fill_z)
    scale = lax.rsqrt(jnp.full((1, 1), norm, f32))

    def fill_root(cols, j):
        for_halves(lambda rows, i: fill_root_half(rows, cols, i, j), half)

    def fill_root_half(rows, cols, i, j):
        eye = eye_tile((half, TILE), i * half, j * TILE)
        v = dot(zh[rows, :], qh[:, cols]) + (
            dot(zh[rows, :], ql[:, cols]) + dot(zl[rows, :], qh[:, cols])
        )
        v = (jnp.where(eye, 2.25, 0.0) - 2.4375 * y[rows, cols] + v) * scale
        root[rows, cols] = v
        rh[rows, cols] = v.astype(bf16)

    tiles(size // TILE, fill_root)
    keep(root, 1)
    acc = jnp.zeros((SLAB, size), f32)
    for d in range(DISTANCES):
        cols = slice(d * SLAB, (d + 1) * SLAB)
        weight = 2.0 if 0 < d < DISTANCES - 1 else 1.0
        high, low = halves(jnp.concatenate([part_a[:, cols], part_b[:, cols]], 0) * weight)
        acc += dot(high, rh[at(z + d), :]) + dot(low, rh[at(z + d), :])
    total = jnp.sum(acc * rh[at(z), :].astype(f32))
    lane = lax.broadcasted_iota(jnp.int32, squares.shape, 2)
    squares[...] = jnp.where(lane == 0, gsq[0, 0], jnp.where(lane == 1, total, 0.0))
    white_copy.wait()
    for out, who in ((own, ids[0]), (other, 1 - ids[0])):
        rows = pl.ds(pl.multiple_of(who * half, half), half)

        def fill(cols, j):
            out[:, cols] = dot(white[rows, :], rh[:, cols])

        tiles(size // TILE, fill)


def root(ids, gsq, pieces, part, wide, rows, peers):
    size = wide.shape[0]
    square = lambda kind: pltpu.VMEM((size, size), kind)
    return call(
        root_kernel,
        [((size // 2, size), f32)] * 2 + [((rows, size), f32), ((peers, 1, 128), f32)],
        [held((size // 2, size))] * 2 + [held((rows, size)), held((peers, 1, 128))],
        [scalar()] + [held(PIECE)] * (len(pieces) + 2) + [pl.BlockSpec(memory_space=pl.ANY)],
        [square(f32)]
        + [square(bf16)] * 7
        + [square(f32), square(bf16), pltpu.SemaphoreType.DMA((1,))],
        44,
        2 * size**3 * 7,
        "root",
    )(ids, gsq, *pieces, *part, wide)


def finish_kernel(ids, squares, own, other, update, kept):
    size = own.shape[1]

    @pl.when(pl.program_id(0) == 0)
    def _():
        sums = jnp.sum(squares[...], axis=0)
        kept[...] = jnp.broadcast_to(
            jnp.sqrt(sums[:, 0:1] / (sums[:, 1:2] + epsilon)), kept.shape
        )

    scale = kept[0:1, 0:1]
    for block, who in ((own, ids[0]), (other, 1 - ids[0])):
        cols = pl.ds(pl.multiple_of(who * size, size), size)
        update[:, cols] = (block[...] * scale).astype(update.dtype)


def finish(ids, squares, own, other):
    rows, size = own.shape
    return pl.pallas_call(
        finish_kernel,
        out_shape=jax.ShapeDtypeStruct((rows, 2 * size), bf16),
        grid_spec=pltpu.PrefetchScalarGridSpec(
            num_scalar_prefetch=1,
            grid=(rows // SLAB,),
            in_specs=[
                pl.BlockSpec(squares.shape, lambda i, s: (0, 0, 0)),
                pl.BlockSpec((SLAB, size), lambda i, s: (i, 0)),
                pl.BlockSpec((SLAB, size), lambda i, s: (i, 0)),
            ],
            out_specs=pl.BlockSpec((SLAB, 2 * size), lambda i, s: (i, 0)),
            scratch_shapes=[pltpu.VMEM((8, 128), f32)],
        ),
        compiler_params=pltpu.CompilerParams(vmem_limit_bytes=16 << 20),
        name="finish",
    )(ids, squares, own, other)


def shift(x, by):
    count = lax.axis_size("z")
    return lax.ppermute(x, "z", [(i, (i + by) % count) for i in range(count)])


def swap(x, axis):
    return lax.ppermute(x, axis, [(0, 1), (1, 0)])


def by_index(which, mine, other, dim):
    return jnp.where(
        which == 0, jnp.concatenate([mine, other], dim), jnp.concatenate([other, mine], dim)
    )


def chip_stats(col_stats, core, z, size):
    rows = col_stats.shape[0]
    mine = lax.dynamic_slice_in_dim(col_stats, core * size, size, 1)
    theirs = lax.dynamic_slice_in_dim(col_stats, (1 - core) * size, size, 1)
    chip = by_index(core, mine, swap(theirs, "core"), 0)
    wide = jnp.concatenate([chip, chip[:, : (DISTANCES - 1) * SLAB]], 1)
    return lax.dynamic_slice(wide, (0, z * SLAB), (2 * rows, DISTANCES * SLAB))


def reduce_ring(pieces):
    def chain(h, first, by):
        sum_ = shift(pieces[2 * first + h], by)
        for k in range(first - by, 0 if by > 0 else 8, -by):
            sum_ = shift(pieces[2 * k + h] + sum_, by)
        return sum_

    up_a, down_b = chain(0, 4, 1), chain(1, 4, -1)
    up_b, down_a = chain(1, 3, 1), chain(0, 5, -1)
    return pieces[0] + up_a + down_a, pieces[1] + up_b + down_b


def gather_ring(own):
    pieces = list(own) + [None] * 14
    for hops in range(4):
        for h, by in ((0, 1), (1, -1), (1, 1), (0, -1)):
            if hops == 3 and (h, by) in ((1, 1), (0, -1)):
                continue
            source = -by * hops % 8
            pieces[2 * (-by * (hops + 1) % 8) + h] = shift(pieces[2 * source + h], by)
    return pieces


def exchange_rows(x, core):
    rows = x.shape[0] // 2
    mine = lax.dynamic_slice_in_dim(x, core * rows, rows, 0)
    theirs = lax.dynamic_slice_in_dim(x, (1 - core) * rows, rows, 0)
    return by_index(core, mine, swap(theirs, "core"), 1)


def shards(acts, grads, row_roots, col_stats):
    size = row_roots.shape[1]
    z, sub, core = lax.axis_index("z"), lax.axis_index("yl"), lax.axis_index("core")
    ids = jnp.stack([core, z, sub]).astype(jnp.int32)
    total_rows = grads.shape[1] * lax.axis_size(("z", "yl", "core"))
    mix = (1.0 - decay_rate) / total_rows

    grads_other, roots_other = swap(grads, "core"), swap(row_roots, "core")
    old = decay_rate * chip_stats(col_stats, core, z, size)
    wide, gsq, *pieces = whiten(ids, acts, grads, grads_other, row_roots, roots_other)
    part = reduce_ring(pieces)
    stats = [mix * part[h] + jnp.where(sub == h, old, 0.0) for h in range(2)]
    stats = [x + swap(x, "yl") for x in stats]
    peers = ("z", "yl", "core", "x", "yh")
    rows = col_stats.shape[0]
    own, other, kept_rows, squares = root(
        ids, gsq, gather_ring(stats), part, wide, 4 * rows, lax.axis_size(peers)
    )
    squares = lax.all_to_all(squares, peers, 0, 0, tiled=True)
    update = finish(ids, squares, own, swap(other, "core"))
    kept_rows = exchange_rows(kept_rows, core)
    return update, kept_rows[:rows], kept_rows[rows:]


def solution(mesh):
    names = ("z", "yl", "core", "x", "yh")
    fine = Mesh(mesh.devices.reshape(8, 2, 2, 4, 2), names)
    row, col = names[:3], names[3:]
    return jax.shard_map(
        shards,
        mesh=fine,
        in_specs=(P(None, col), P(None, row), P(row, None), P(row, col)),
        out_specs=(P(row, col), P(row, col), P(row, col)),
        check_vma=False,
    )
```

```python
import jax
import jax.numpy as jnp
from jax import lax
from jax.sharding import Mesh, PartitionSpec as P
from jax.experimental import pallas as pl
from jax.experimental.pallas import tpu as pltpu

decay_rate = 0.75
damping = 0.001
epsilon = 1e-06
TILE = 256
SLAB = 128
DISTANCES = 5
f32 = jnp.float32
bf16 = jnp.bfloat16


def tdot(a, b):
    return lax.dot_general(a, b, (((0,), (0,)), ((), ())), preferred_element_type=f32)


def dot(a, b):
    return jnp.dot(a, b, preferred_element_type=f32)


def tiles(count, body):
    def turn(j, carry):
        body(pl.ds(pl.multiple_of(j * TILE, TILE), TILE), j)
        return carry

    lax.fori_loop(0, count, turn, 0)


def held(shape, index=None):
    index = index or (lambda i, s: (0,) * len(shape))
    return pl.BlockSpec(shape, index, pipeline_mode=pl.Buffered(1))


def scalar():
    return pl.BlockSpec(memory_space=pltpu.SMEM)


def call(kernel, outs, out_specs, in_specs, scratch, limit, flops, name):
    return pl.pallas_call(
        kernel,
        out_shape=[jax.ShapeDtypeStruct(*o) for o in outs],
        grid_spec=pltpu.PrefetchScalarGridSpec(
            num_scalar_prefetch=1,
            grid=(1,),
            in_specs=in_specs,
            out_specs=out_specs,
            scratch_shapes=scratch,
        ),
        compiler_params=pltpu.CompilerParams(vmem_limit_bytes=limit << 20),
        cost_estimate=pl.CostEstimate(flops=flops, bytes_accessed=8 << 20, transcendentals=0),
        name=name,
    )


def slab(ids, k):
    return lax.rem(ids[1] + k, 8)


def whiten_kernel(ids, acts, g_own, g_other, r_own, r_other, wide, gsq, *rest):
    pieces, (block, g, turned, r, grad, tile_sems, sems) = rest[:-7], rest[-7:]
    core = ids[0]
    half = g_own.shape[1]
    size = block.shape[1]
    cut = SLAB // 2

    def tile_copy(j):
        source = pl.ds(pl.multiple_of(core * size + j * TILE, TILE), TILE)
        target = pl.ds(pl.multiple_of(j * TILE, TILE), TILE)
        return pltpu.make_async_copy(acts.at[:, source], block.at[:, target], tile_sems.at[j])

    copies = [
        pltpu.make_async_copy(source, target, sems.at[i])
        for i, (source, target) in enumerate(
            ((g_own, g.at[0]), (g_other, g.at[1]), (r_own, r.at[0]), (r_other, r.at[1]))
        )
    ]
    copies[0].start()
    for j in range(size // TILE):
        tile_copy(j).start()
    for copy in copies[1:]:
        copy.start()
    gsq[0, 0] = 0.0
    for i, who in enumerate((core, 1 - core)):
        first = pl.multiple_of(who * half, half)
        copies[i].wait()
        turned[...] = g[i].T

        def fill_grad(cols, j):
            if i == 0:
                tile_copy(j).wait()
            t = dot(turned[...], block[:, cols]).astype(bf16)
            grad[pl.ds(first, half), cols] = t
            gsq[0, 0] += jnp.sum(jnp.square(t.astype(f32)))

        tiles(size // TILE, fill_grad)
    for i, who in enumerate((core, 1 - core)):
        first = pl.multiple_of(who * half, half)
        copies[2 + i].wait()

        def fill_white(cols, j):
            wide[pl.ds(first, half), cols] = dot(r[i], grad[:, cols]).astype(bf16)

        tiles(size // TILE, fill_white)
    wide[:, size:] = wide[:, : DISTANCES * SLAB]
    span = DISTANCES * SLAB
    for k in range(0, size // SLAB, 2):
        first = pl.multiple_of(slab(ids, k) * SLAB, SLAB)
        t = tdot(wide[:, pl.ds(first, 2 * SLAB)], wide[:, pl.ds(first, span + SLAB)])
        for i in range(4):
            left = i // 2 * SLAB
            pieces[2 * k + i][...] = t[i * cut : (i + 1) * cut, left : left + span]


WHITEN_MIB = 51
PIECE = (SLAB // 2, DISTANCES * SLAB)


def whiten(ids, acts, g_own, g_other, r_own, r_other):
    tok, half = g_own.shape
    size = r_own.shape[1]
    count = 2 * size // SLAB
    wide = (size, size + DISTANCES * SLAB)
    return call(
        whiten_kernel,
        [(wide, bf16), ((1, 1), f32)] + [(PIECE, f32)] * count,
        [held(wide), scalar()] + [held(PIECE)] * count,
        [pl.BlockSpec(memory_space=pl.ANY)] * 5,
        [
            pltpu.VMEM((tok, size), bf16),
            pltpu.VMEM((2, tok, half), bf16),
            pltpu.VMEM((half, tok), bf16),
            pltpu.VMEM((2, half, size), bf16),
            pltpu.VMEM((size, size), bf16),
            pltpu.SemaphoreType.DMA((size // TILE,)),
            pltpu.SemaphoreType.DMA((4,)),
        ],
        WHITEN_MIB,
        2 * size * size * (tok + size + DISTANCES * SLAB),
        "whiten",
    )(ids, acts, g_own, g_other, r_own, r_other)


def halves(x):
    high = x.astype(bf16)
    return high, (x - high.astype(f32)).astype(bf16)


def eye_tile(shape, row, col):
    return (
        lax.broadcasted_iota(jnp.int32, shape, 0) + row
        == lax.broadcasted_iota(jnp.int32, shape, 1) + col
    )


def root_kernel(ids, gsq, *refs):
    slabs = 8
    pieces = refs[: 2 * slabs]
    part_a, part_b, wide, own, other, kept_rows, squares = refs[2 * slabs : 2 * slabs + 7]
    y, yh, yl, zh, zl, qh, ql, rh, root, white, white_sem = refs[2 * slabs + 7 :]
    white_copy = pltpu.make_async_copy(wide.at[:, pl.ds(0, rh.shape[1])], white, white_sem.at[0])
    white_copy.start()
    z, sub = ids[1], ids[2]
    size = rh.shape[1]
    cut = SLAB // 2
    quarter = kept_rows.shape[0] // 4

    def keep(source, place):
        for core in range(2):
            first = z * SLAB + (2 * sub + core) * quarter
            kept_rows[pl.ds((2 * core + place) * quarter, quarter), :] = source[
                pl.ds(pl.multiple_of(first, quarter), quarter), :
            ]


    def at(k):
        return pl.ds(pl.multiple_of(lax.rem(k, slabs) * SLAB, SLAB), SLAB)

    diagonal = eye_tile((SLAB, SLAB), 0, 0)
    trace = jnp.float32(0)
    for k in range(slabs):
        q = slab(ids, k)
        for d in range(DISTANCES):
            cols = slice(d * SLAB, (d + 1) * SLAB)
            block = jnp.concatenate([pieces[2 * k][:, cols], pieces[2 * k + 1][:, cols]], 0)
            y[at(q), at(q + d)] = block
            if d == 0:
                trace += jnp.sum(jnp.where(diagonal, block + damping, 0.0))
            elif d < DISTANCES - 1:
                y[at(q + d), at(q)] = block.T
    keep(y, 0)
    norm = 2.0 * trace / size
    inverse = 1.0 / norm

    def fill_y(rows, i):
        eye = eye_tile((TILE, size), i * TILE, 0)
        v = (y[rows, :] + jnp.where(eye, damping, 0.0)) * inverse
        y[rows, :] = v
        yh[rows, :], yl[rows, :] = halves(v)

    tiles(size // TILE, fill_y)

    half = size // 2

    def fill_z(cols, j):
        eye = eye_tile((size, TILE), 0, j * TILE)
        v = dot(yh[...], yh[:, cols]) + (dot(yh[...], yl[:, cols]) + dot(yl[...], yh[:, cols]))
        zh[:, cols], zl[:, cols] = halves(v)
        q = jnp.where(eye, 1.6875, 0.0) - 0.5625 * y[:, cols] + 0.0625 * v
        qh[:, cols], ql[:, cols] = halves(q)

    tiles(size // TILE, fill_z)
    scale = lax.rsqrt(jnp.full((1, 1), norm, f32))

    def fill_root(cols, j):
        eye = eye_tile((size, TILE), 0, j * TILE)
        v = dot(zh[...], qh[:, cols]) + (dot(zh[...], ql[:, cols]) + dot(zl[...], qh[:, cols]))
        v = (jnp.where(eye, 2.25, 0.0) - 2.4375 * y[:, cols] + v) * scale
        root[:, cols] = v
        rh[:, cols] = v.astype(bf16)

    tiles(size // TILE, fill_root)
    keep(root, 1)
    acc = jnp.zeros((SLAB, size), f32)
    for d in range(DISTANCES):
        cols = slice(d * SLAB, (d + 1) * SLAB)
        weight = 2.0 if 0 < d < DISTANCES - 1 else 1.0
        high, low = halves(jnp.concatenate([part_a[:, cols], part_b[:, cols]], 0) * weight)
        acc += dot(high, rh[at(z + d), :]) + dot(low, rh[at(z + d), :])
    total = jnp.sum(acc * rh[at(z), :].astype(f32))
    lane = lax.broadcasted_iota(jnp.int32, squares.shape, 2)
    squares[...] = jnp.where(lane == 0, gsq[0, 0], jnp.where(lane == 1, total, 0.0))
    white_copy.wait()
    for out, who in ((own, ids[0]), (other, 1 - ids[0])):
        rows = pl.ds(pl.multiple_of(who * half, half), half)

        def fill(cols, j):
            out[:, cols] = dot(white[rows, :], rh[:, cols])

        tiles(size // TILE, fill)


def root(ids, gsq, pieces, part, wide, rows, peers):
    size = wide.shape[0]
    square = lambda kind: pltpu.VMEM((size, size), kind)
    return call(
        root_kernel,
        [((size // 2, size), f32)] * 2 + [((rows, size), f32), ((peers, 1, 128), f32)],
        [held((size // 2, size))] * 2 + [held((rows, size)), held((peers, 1, 128))],
        [scalar()] + [held(PIECE)] * (len(pieces) + 2) + [pl.BlockSpec(memory_space=pl.ANY)],
        [square(f32)]
        + [square(bf16)] * 7
        + [square(f32), square(bf16), pltpu.SemaphoreType.DMA((1,))],
        44,
        2 * size**3 * 7,
        "root",
    )(ids, gsq, *pieces, *part, wide)


def finish_kernel(ids, squares, own, other, update, kept):
    size = own.shape[1]

    @pl.when(pl.program_id(0) == 0)
    def _():
        sums = jnp.sum(squares[...], axis=0)
        kept[...] = jnp.broadcast_to(
            jnp.sqrt(sums[:, 0:1] / (sums[:, 1:2] + epsilon)), kept.shape
        )

    scale = kept[0:1, 0:1]
    for block, who in ((own, ids[0]), (other, 1 - ids[0])):
        cols = pl.ds(pl.multiple_of(who * size, size), size)
        update[:, cols] = (block[...] * scale).astype(update.dtype)


def finish(ids, squares, own, other):
    rows, size = own.shape
    return pl.pallas_call(
        finish_kernel,
        out_shape=jax.ShapeDtypeStruct((rows, 2 * size), bf16),
        grid_spec=pltpu.PrefetchScalarGridSpec(
            num_scalar_prefetch=1,
            grid=(rows // SLAB,),
            in_specs=[
                pl.BlockSpec(squares.shape, lambda i, s: (0, 0, 0)),
                pl.BlockSpec((SLAB, size), lambda i, s: (i, 0)),
                pl.BlockSpec((SLAB, size), lambda i, s: (i, 0)),
            ],
            out_specs=pl.BlockSpec((SLAB, 2 * size), lambda i, s: (i, 0)),
            scratch_shapes=[pltpu.VMEM((8, 128), f32)],
        ),
        compiler_params=pltpu.CompilerParams(vmem_limit_bytes=16 << 20),
        name="finish",
    )(ids, squares, own, other)


def shift(x, by):
    count = lax.axis_size("z")
    return lax.ppermute(x, "z", [(i, (i + by) % count) for i in range(count)])


def swap(x, axis):
    return lax.ppermute(x, axis, [(0, 1), (1, 0)])


def by_index(which, mine, other, dim):
    return jnp.where(
        which == 0, jnp.concatenate([mine, other], dim), jnp.concatenate([other, mine], dim)
    )


def chip_stats(col_stats, core, z, size):
    rows = col_stats.shape[0]
    mine = lax.dynamic_slice_in_dim(col_stats, core * size, size, 1)
    theirs = lax.dynamic_slice_in_dim(col_stats, (1 - core) * size, size, 1)
    chip = by_index(core, mine, swap(theirs, "core"), 0)
    wide = jnp.concatenate([chip, chip[:, : (DISTANCES - 1) * SLAB]], 1)
    return lax.dynamic_slice(wide, (0, z * SLAB), (2 * rows, DISTANCES * SLAB))


def reduce_ring(pieces):
    def chain(h, first, by):
        sum_ = shift(pieces[2 * first + h], by)
        for k in range(first - by, 0 if by > 0 else 8, -by):
            sum_ = shift(pieces[2 * k + h] + sum_, by)
        return sum_

    up_a, down_b = chain(0, 4, 1), chain(1, 4, -1)
    up_b, down_a = chain(1, 3, 1), chain(0, 5, -1)
    return pieces[0] + up_a + down_a, pieces[1] + up_b + down_b


def gather_ring(own):
    pieces = list(own) + [None] * 14
    for hops in range(4):
        for h, by in ((0, 1), (1, -1), (1, 1), (0, -1)):
            if hops == 3 and (h, by) in ((1, 1), (0, -1)):
                continue
            source = -by * hops % 8
            pieces[2 * (-by * (hops + 1) % 8) + h] = shift(pieces[2 * source + h], by)
    return pieces


def exchange_rows(x, core):
    rows = x.shape[0] // 2
    mine = lax.dynamic_slice_in_dim(x, core * rows, rows, 0)
    theirs = lax.dynamic_slice_in_dim(x, (1 - core) * rows, rows, 0)
    return by_index(core, mine, swap(theirs, "core"), 1)


def shards(acts, grads, row_roots, col_stats):
    size = row_roots.shape[1]
    z, sub, core = lax.axis_index("z"), lax.axis_index("yl"), lax.axis_index("core")
    ids = jnp.stack([core, z, sub]).astype(jnp.int32)
    total_rows = grads.shape[1] * lax.axis_size(("z", "yl", "core"))
    mix = (1.0 - decay_rate) / total_rows

    grads_other, roots_other = swap(grads, "core"), swap(row_roots, "core")
    old = decay_rate * chip_stats(col_stats, core, z, size)
    wide, gsq, *pieces = whiten(ids, acts, grads, grads_other, row_roots, roots_other)
    part = reduce_ring(pieces)
    stats = [mix * part[h] + jnp.where(sub == h, old, 0.0) for h in range(2)]
    stats = [x + swap(x, "yl") for x in stats]
    peers = ("z", "yl", "core", "x", "yh")
    rows = col_stats.shape[0]
    own, other, kept_rows, squares = root(
        ids, gsq, gather_ring(stats), part, wide, 4 * rows, lax.axis_size(peers)
    )
    squares = lax.all_to_all(squares, peers, 0, 0, tiled=True)
    update = finish(ids, squares, own, swap(other, "core"))
    kept_rows = exchange_rows(kept_rows, core)
    return update, kept_rows[:rows], kept_rows[rows:]


def solution(mesh):
    names = ("z", "yl", "core", "x", "yh")
    fine = Mesh(mesh.devices.reshape(8, 2, 2, 4, 2), names)
    row, col = names[:3], names[3:]
    return jax.shard_map(
        shards,
        mesh=fine,
        in_specs=(P(None, col), P(None, row), P(row, None), P(row, col)),
        out_specs=(P(row, col), P(row, col), P(row, col)),
        check_vma=False,
    )
```

```python
import jax
import jax.numpy as jnp
from jax import lax
from jax.sharding import Mesh, PartitionSpec as P
from jax.experimental import pallas as pl
from jax.experimental.pallas import tpu as pltpu

decay_rate = 0.75
damping = 0.001
epsilon = 1e-06
TILE = 256
WIDE = 512
SLAB = 128
DISTANCES = 5
f32 = jnp.float32
bf16 = jnp.bfloat16


def tdot(a, b):
    return lax.dot_general(a, b, (((0,), (0,)), ((), ())), preferred_element_type=f32)


def dot(a, b):
    return jnp.dot(a, b, preferred_element_type=f32)


def tiles(count, body, step=TILE):
    def turn(j, carry):
        body(pl.ds(pl.multiple_of(j * step, step), step), j)
        return carry

    lax.fori_loop(0, count, turn, 0)


def held(shape, index=None):
    index = index or (lambda i, s: (0,) * len(shape))
    return pl.BlockSpec(shape, index, pipeline_mode=pl.Buffered(1))


def scalar():
    return pl.BlockSpec(memory_space=pltpu.SMEM)


def call(kernel, outs, out_specs, in_specs, scratch, limit, flops, name):
    return pl.pallas_call(
        kernel,
        out_shape=[jax.ShapeDtypeStruct(*o) for o in outs],
        grid_spec=pltpu.PrefetchScalarGridSpec(
            num_scalar_prefetch=1,
            grid=(1,),
            in_specs=in_specs,
            out_specs=out_specs,
            scratch_shapes=scratch,
        ),
        compiler_params=pltpu.CompilerParams(vmem_limit_bytes=limit << 20),
        cost_estimate=pl.CostEstimate(flops=flops, bytes_accessed=8 << 20, transcendentals=0),
        name=name,
    )


def slab(ids, k):
    return lax.rem(ids[1] + k, 8)


def whiten_kernel(ids, acts, g_own, g_other, r_own, r_other, wide, gsq, *rest):
    pieces, (block, g, r, grad, summed, tile_sems, sems) = rest[:-7], rest[-7:]
    core = ids[0]
    half = g_own.shape[1]
    size = block.shape[1]
    cut = SLAB // 2

    def tile_copy(j):
        source = pl.ds(pl.multiple_of(core * size + j * WIDE, WIDE), WIDE)
        target = pl.ds(pl.multiple_of(j * WIDE, WIDE), WIDE)
        return pltpu.make_async_copy(acts.at[:, source], block.at[:, target], tile_sems.at[j])

    copies = [
        pltpu.make_async_copy(source, target, sems.at[i])
        for i, (source, target) in enumerate(
            ((g_own, g.at[0]), (g_other, g.at[1]), (r_own, r.at[0]), (r_other, r.at[1]))
        )
    ]
    copies[0].start()
    for j in range(size // WIDE):
        tile_copy(j).start()
    for copy in copies[1:]:
        copy.start()
    summed[...] = jnp.zeros_like(summed)
    for i, who in enumerate((core, 1 - core)):
        first = pl.multiple_of(who * half, half)
        copies[i].wait()

        def fill_grad(cols, j):
            if i == 0:
                tile_copy(j).wait()
            t = tdot(g[i], block[:, cols]).astype(bf16)
            grad[pl.ds(first, half), cols] = t
            squares = jnp.square(t.astype(f32)).reshape(half // 8, 8, WIDE)
            summed[...] += jnp.sum(squares, axis=0)

        tiles(size // WIDE, fill_grad, WIDE)
    for i, who in enumerate((core, 1 - core)):
        first = pl.multiple_of(who * half, half)
        copies[2 + i].wait()

        def fill_white(cols, j):
            wide[pl.ds(first, half), cols] = dot(r[i], grad[:, cols]).astype(bf16)

        tiles(size // WIDE, fill_white, WIDE)
    gsq[0, 0] = jnp.sum(summed[...])
    wide[:, size:] = wide[:, : DISTANCES * SLAB]
    span = DISTANCES * SLAB
    for k in range(0, size // SLAB, 2):
        first = pl.multiple_of(slab(ids, k) * SLAB, SLAB)
        t = tdot(wide[:, pl.ds(first, 2 * SLAB)], wide[:, pl.ds(first, span + SLAB)])
        for i in range(4):
            left = i // 2 * SLAB
            pieces[2 * k + i][...] = t[i * cut : (i + 1) * cut, left : left + span]


WHITEN_MIB = 51
PIECE = (SLAB // 2, DISTANCES * SLAB)


def whiten(ids, acts, g_own, g_other, r_own, r_other):
    tok, half = g_own.shape
    size = r_own.shape[1]
    count = 2 * size // SLAB
    wide = (size, size + DISTANCES * SLAB)
    return call(
        whiten_kernel,
        [(wide, bf16), ((1, 1), f32)] + [(PIECE, f32)] * count,
        [held(wide), scalar()] + [held(PIECE)] * count,
        [pl.BlockSpec(memory_space=pl.ANY)] * 5,
        [
            pltpu.VMEM((tok, size), bf16),
            pltpu.VMEM((2, tok, half), bf16),
            pltpu.VMEM((2, half, size), bf16),
            pltpu.VMEM((size, size), bf16),
            pltpu.VMEM((8, WIDE), f32),
            pltpu.SemaphoreType.DMA((size // WIDE,)),
            pltpu.SemaphoreType.DMA((4,)),
        ],
        WHITEN_MIB,
        2 * size * size * (tok + size + DISTANCES * SLAB),
        "whiten",
    )(ids, acts, g_own, g_other, r_own, r_other)


def halves(x):
    high = x.astype(bf16)
    return high, (x - high.astype(f32)).astype(bf16)


def eye_tile(shape, row, col):
    return (
        lax.broadcasted_iota(jnp.int32, shape, 0) + row
        == lax.broadcasted_iota(jnp.int32, shape, 1) + col
    )


def root_kernel(ids, gsq, *refs):
    slabs = 8
    pieces = refs[: 2 * slabs]
    part_a, part_b, wide, own, other, kept_rows, squares = refs[2 * slabs : 2 * slabs + 7]
    y, yh, yl, zh, zl, qh, ql, rh, root, white, white_sem = refs[2 * slabs + 7 :]
    white_copy = pltpu.make_async_copy(wide.at[:, pl.ds(0, rh.shape[1])], white, white_sem.at[0])
    white_copy.start()
    z, sub = ids[1], ids[2]
    size = rh.shape[1]
    cut = SLAB // 2
    quarter = kept_rows.shape[0] // 4

    def keep(source, place):
        for core in range(2):
            first = z * SLAB + (2 * sub + core) * quarter
            kept_rows[pl.ds((2 * core + place) * quarter, quarter), :] = source[
                pl.ds(pl.multiple_of(first, quarter), quarter), :
            ]


    def at(k):
        return pl.ds(pl.multiple_of(lax.rem(k, slabs) * SLAB, SLAB), SLAB)

    diagonal = eye_tile((SLAB, SLAB), 0, 0)
    trace = jnp.float32(0)
    for k in range(slabs):
        q = slab(ids, k)
        for d in range(DISTANCES):
            cols = slice(d * SLAB, (d + 1) * SLAB)
            block = jnp.concatenate([pieces[2 * k][:, cols], pieces[2 * k + 1][:, cols]], 0)
            y[at(q), at(q + d)] = block
            if d == 0:
                trace += jnp.sum(jnp.where(diagonal, block + damping, 0.0))
            elif d < DISTANCES - 1:
                y[at(q + d), at(q)] = block.T
    keep(y, 0)
    norm = 2.0 * trace / size
    inverse = 1.0 / norm

    def fill_y(rows, i):
        eye = eye_tile((TILE, size), i * TILE, 0)
        v = (y[rows, :] + jnp.where(eye, damping, 0.0)) * inverse
        y[rows, :] = v
        yh[rows, :], yl[rows, :] = halves(v)

    tiles(size // TILE, fill_y)

    half = size // 2

    def fill_z(cols, j):
        eye = eye_tile((size, TILE), 0, j * TILE)
        v = dot(yh[...], yh[:, cols]) + (dot(yh[...], yl[:, cols]) + dot(yl[...], yh[:, cols]))
        zh[:, cols], zl[:, cols] = halves(v)
        q = jnp.where(eye, 1.6875, 0.0) - 0.5625 * y[:, cols] + 0.0625 * v
        qh[:, cols], ql[:, cols] = halves(q)

    tiles(size // TILE, fill_z)
    scale = lax.rsqrt(jnp.full((1, 1), norm, f32))

    def fill_root(cols, j):
        eye = eye_tile((size, TILE), 0, j * TILE)
        v = dot(zh[...], qh[:, cols]) + (dot(zh[...], ql[:, cols]) + dot(zl[...], qh[:, cols]))
        v = (jnp.where(eye, 2.25, 0.0) - 2.4375 * y[:, cols] + v) * scale
        root[:, cols] = v
        rh[:, cols] = v.astype(bf16)

    tiles(size // TILE, fill_root)
    keep(root, 1)
    acc = jnp.zeros((SLAB, size), f32)
    for d in range(DISTANCES):
        cols = slice(d * SLAB, (d + 1) * SLAB)
        weight = 2.0 if 0 < d < DISTANCES - 1 else 1.0
        high, low = halves(jnp.concatenate([part_a[:, cols], part_b[:, cols]], 0) * weight)
        acc += dot(high, rh[at(z + d), :]) + dot(low, rh[at(z + d), :])
    total = jnp.sum(acc * rh[at(z), :].astype(f32))
    lane = lax.broadcasted_iota(jnp.int32, squares.shape, 2)
    squares[...] = jnp.where(lane == 0, gsq[0, 0], jnp.where(lane == 1, total, 0.0))
    white_copy.wait()
    for out, who in ((own, ids[0]), (other, 1 - ids[0])):
        rows = pl.ds(pl.multiple_of(who * half, half), half)

        def fill(cols, j):
            out[:, cols] = dot(white[rows, :], rh[:, cols])

        tiles(size // TILE, fill)


def root(ids, gsq, pieces, part, wide, rows, peers):
    size = wide.shape[0]
    square = lambda kind: pltpu.VMEM((size, size), kind)
    return call(
        root_kernel,
        [((size // 2, size), f32)] * 2 + [((rows, size), f32), ((peers, 1, 128), f32)],
        [held((size // 2, size))] * 2 + [held((rows, size)), held((peers, 1, 128))],
        [scalar()] + [held(PIECE)] * (len(pieces) + 2) + [pl.BlockSpec(memory_space=pl.ANY)],
        [square(f32)]
        + [square(bf16)] * 7
        + [square(f32), square(bf16), pltpu.SemaphoreType.DMA((1,))],
        44,
        2 * size**3 * 7,
        "root",
    )(ids, gsq, *pieces, *part, wide)


def finish_kernel(ids, squares, own, other, update, kept):
    size = own.shape[1]

    @pl.when(pl.program_id(0) == 0)
    def _():
        sums = jnp.sum(squares[...], axis=0)
        kept[...] = jnp.broadcast_to(
            jnp.sqrt(sums[:, 0:1] / (sums[:, 1:2] + epsilon)), kept.shape
        )

    scale = kept[0:1, 0:1]
    for block, who in ((own, ids[0]), (other, 1 - ids[0])):
        cols = pl.ds(pl.multiple_of(who * size, size), size)
        update[:, cols] = (block[...] * scale).astype(update.dtype)


def finish(ids, squares, own, other):
    rows, size = own.shape
    return pl.pallas_call(
        finish_kernel,
        out_shape=jax.ShapeDtypeStruct((rows, 2 * size), bf16),
        grid_spec=pltpu.PrefetchScalarGridSpec(
            num_scalar_prefetch=1,
            grid=(rows // SLAB,),
            in_specs=[
                pl.BlockSpec(squares.shape, lambda i, s: (0, 0, 0)),
                pl.BlockSpec((SLAB, size), lambda i, s: (i, 0)),
                pl.BlockSpec((SLAB, size), lambda i, s: (i, 0)),
            ],
            out_specs=pl.BlockSpec((SLAB, 2 * size), lambda i, s: (i, 0)),
            scratch_shapes=[pltpu.VMEM((8, 128), f32)],
        ),
        compiler_params=pltpu.CompilerParams(vmem_limit_bytes=16 << 20),
        name="finish",
    )(ids, squares, own, other)


def shift(x, by):
    count = lax.axis_size("z")
    return lax.ppermute(x, "z", [(i, (i + by) % count) for i in range(count)])


def swap(x, axis):
    return lax.ppermute(x, axis, [(0, 1), (1, 0)])


def by_index(which, mine, other, dim):
    return jnp.where(
        which == 0, jnp.concatenate([mine, other], dim), jnp.concatenate([other, mine], dim)
    )


def chip_stats(col_stats, core, z, size):
    rows = col_stats.shape[0]
    mine = lax.dynamic_slice_in_dim(col_stats, core * size, size, 1)
    theirs = lax.dynamic_slice_in_dim(col_stats, (1 - core) * size, size, 1)
    chip = by_index(core, mine, swap(theirs, "core"), 0)
    wide = jnp.concatenate([chip, chip[:, : (DISTANCES - 1) * SLAB]], 1)
    return lax.dynamic_slice(wide, (0, z * SLAB), (2 * rows, DISTANCES * SLAB))


def reduce_ring(pieces):
    def chain(h, first, by):
        sum_ = shift(pieces[2 * first + h], by)
        for k in range(first - by, 0 if by > 0 else 8, -by):
            sum_ = shift(pieces[2 * k + h] + sum_, by)
        return sum_

    up_a, down_b = chain(0, 4, 1), chain(1, 4, -1)
    up_b, down_a = chain(1, 3, 1), chain(0, 5, -1)
    return pieces[0] + up_a + down_a, pieces[1] + up_b + down_b


def gather_ring(own):
    pieces = list(own) + [None] * 14
    for hops in range(4):
        for h, by in ((0, 1), (1, -1), (1, 1), (0, -1)):
            if hops == 3 and (h, by) in ((1, 1), (0, -1)):
                continue
            source = -by * hops % 8
            pieces[2 * (-by * (hops + 1) % 8) + h] = shift(pieces[2 * source + h], by)
    return pieces


def exchange_rows(x, core):
    rows = x.shape[0] // 2
    mine = lax.dynamic_slice_in_dim(x, core * rows, rows, 0)
    theirs = lax.dynamic_slice_in_dim(x, (1 - core) * rows, rows, 0)
    return by_index(core, mine, swap(theirs, "core"), 1)


def shards(acts, grads, row_roots, col_stats):
    size = row_roots.shape[1]
    z, sub, core = lax.axis_index("z"), lax.axis_index("yl"), lax.axis_index("core")
    ids = jnp.stack([core, z, sub]).astype(jnp.int32)
    total_rows = grads.shape[1] * lax.axis_size(("z", "yl", "core"))
    mix = (1.0 - decay_rate) / total_rows

    grads_other, roots_other = swap(grads, "core"), swap(row_roots, "core")
    old = decay_rate * chip_stats(col_stats, core, z, size)
    wide, gsq, *pieces = whiten(ids, acts, grads, grads_other, row_roots, roots_other)
    part = reduce_ring(pieces)
    stats = [mix * part[h] + jnp.where(sub == h, old, 0.0) for h in range(2)]
    stats = [x + swap(x, "yl") for x in stats]
    peers = ("z", "yl", "core", "x", "yh")
    rows = col_stats.shape[0]
    own, other, kept_rows, squares = root(
        ids, gsq, gather_ring(stats), part, wide, 4 * rows, lax.axis_size(peers)
    )
    squares = lax.all_to_all(squares, peers, 0, 0, tiled=True)
    update = finish(ids, squares, own, swap(other, "core"))
    kept_rows = exchange_rows(kept_rows, core)
    return update, kept_rows[:rows], kept_rows[rows:]


def solution(mesh):
    names = ("z", "yl", "core", "x", "yh")
    fine = Mesh(mesh.devices.reshape(8, 2, 2, 4, 2), names)
    row, col = names[:3], names[3:]
    return jax.shard_map(
        shards,
        mesh=fine,
        in_specs=(P(None, col), P(None, row), P(row, None), P(row, col)),
        out_specs=(P(row, col), P(row, col), P(row, col)),
        check_vma=False,
    )
```
